256 devices in a mesh: row: 32 (over x, y, core), col: 8 (over z).
Axes of the slice: x: 4, y: 4, z: 8, core: 2. Of those that a mesh axis runs over, the one named last changes fastest.
Arguments:
- matrix: float32 [65536, 5, 8, 128], P('row', None, 'col'), may hold values from -320 to 320, as said below
Outputs:
- r_rows: float32 [256, 5, 8, 128], P(None, None, 'col')
- residual: float32 [65536, 5, 8, 128], P('row', None, 'col')
The draws below stay inside these ranges and needn't reach their ends.
Inputs may be any that keep to these rules, and one draw needn't show every extreme that they name: `matrix`: real entries; the first 256 columns have full column rank on every block of 2048 rows.
All inputs are finite; a program needn't handle non-finite values.
Results may differ from the reference program's by a relative error of at most 0.0003.
Values sent between devices are 32-bit elements; how exact they have to be, the bound alone decides.
No kernel may reach another device: no remote copies, remote signals or barrier semaphores. Data moves between devices by JAX's collectives and lax.ppermute only.
A program may use at most 128 MiB of HBM per device.

```python
import math
import jax
import jax.numpy as jnp
from jax import lax

BLK = 128
PANEL = 256
CB = 5
ROWS = 65536
N_COL = 8


def draw_matrix(key, part):
    key_base = jax.random.fold_in(key, 11)
    key_gain = jax.random.fold_in(key, 12)
    key_scale = jax.random.fold_in(key, 13)
    shape = (ROWS, CB, N_COL, BLK)
    base = jax.random.truncated_normal(key_base, -4.0, 4.0, shape, jnp.float32)
    first = base[:, 0, 0:2, :].reshape(ROWS, PANEL)
    mixed = first + 0.6 * jnp.roll(first, -1, axis=1)
    mixed_blocks = mixed.reshape(ROWS, 2, BLK)
    parity = jnp.arange(N_COL) % 2
    spread = mixed_blocks[:, parity, :][:, None, :, :]
    gains = jax.random.uniform(key_gain, (CB, N_COL, BLK), jnp.float32, -1.0, 1.0)
    full = base + gains[None] * spread
    full = full.at[:, 0, 0:2, :].set(mixed_blocks)
    rising = jnp.arange(ROWS, dtype=jnp.float32) / ROWS
    jitter = jax.random.uniform(key_scale, (ROWS,), jnp.float32, 0.0, 1.0)
    scales = jnp.exp(math.log(3.0) * rising + math.log(10.0) * jitter)
    return (full * scales[:, None, None, None]).astype(jnp.float32)


def setup_inputs(seed: int = 0) -> dict:
    keys = jax.random.split(jax.random.key(seed), 2)
    return {
        "matrix": draw_matrix(jax.random.fold_in(keys[1], 71), 0),
    }


def reference(matrix):
    flat = matrix.reshape(ROWS, CB * N_COL * BLK)
    panel = flat[:, :PANEL]
    basis, upper = jnp.linalg.qr(panel)
    signs = jnp.where(jnp.diagonal(upper) < 0, -1.0, 1.0)
    basis = basis * signs[None, :]
    top = jnp.dot(basis.T, flat, precision=lax.Precision.HIGHEST)
    residual = flat - jnp.dot(basis, top, precision=lax.Precision.HIGHEST)
    scaled = top / math.sqrt(ROWS)
    return (scaled.reshape(PANEL, CB, N_COL, BLK), residual.reshape(ROWS, CB, N_COL, BLK))
```

```python
import functools
import math

import jax
import jax.numpy as jnp
from jax import lax
from jax.experimental import pallas as pl
from jax.experimental.pallas import tpu as pltpu
from jax.sharding import PartitionSpec as P

LANES = 128
STEP = 32
GROUP = 4
HIGHEST = lax.Precision.HIGHEST


def split(value):
    high = value.astype(jnp.bfloat16)
    low = (value - high.astype(jnp.float32)).astype(jnp.bfloat16)
    return high, low


def contract(left, right, dims, precision=None):
    return lax.dot_general(
        left, right, (dims, ((), ())), precision=precision, preferred_element_type=jnp.float32
    )


def dot3(left, right, dims):
    (lh, ll), (rh, rl) = left, right
    return contract(lh, rh, dims) + (contract(lh, rl, dims) + contract(ll, rh, dims))


def piece_order(col, n_col):
    half = n_col // 2
    order = [col]
    for hop in range(1, half):
        order.append(lax.rem(col + n_col - hop, n_col))
        order.append(lax.rem(col + hop, n_col))
    order.append(lax.rem(col + half, n_col))
    return order


def load_piece(ref):
    rows = ref.shape[0] // 2
    return jnp.concatenate([ref[:rows], ref[rows:]], axis=1)


def products_kernel(n_col, blocks, where_ref, *refs):
    pieces, matrix_ref = refs[:n_col], refs[n_col]
    gram_ref, cross_ref, window, sems = refs[n_col + 1 :]
    order = piece_order(where_ref[0], n_col)
    rows = pieces[0].shape[0] // 2
    copies = []
    for spot in range(n_col):
        start = pl.multiple_of(order[spot] * (rows * blocks), rows * blocks)
        copy = pltpu.make_async_copy(
            matrix_ref.at[pl.ds(start, rows * blocks)], window.at[spot], sems.at[spot]
        )
        copy.start()
        copies.append(copy)
    first = ((0,), (0,))
    for spot in range(n_col):
        panel = load_piece(pieces[spot])
        parts = split(panel)
        gram = contract(panel, panel, first, HIGHEST)
        copies[spot].wait()
        for half in range(2):
            term = gram[:, half * LANES : (half + 1) * LANES]
            if spot == 0:
                gram_ref[half] = term
            else:
                gram_ref[half] += term
        for block in range(blocks):
            local = split(window[spot, pl.ds(block, rows, stride=blocks), :])
            term = dot3(parts, local, first)
            if spot == 0:
                cross_ref[block] = term
            else:
                cross_ref[block] += term


def factor_kernel(where_ref, mine_ref, other_ref, out_ref, work):
    size = work.shape[0]
    core = where_ref[1]

    @pl.when(core == 0)
    def _():
        work[:, :LANES] = mine_ref[...]
        work[:, LANES:] = other_ref[...]

    @pl.when(core != 0)
    def _():
        work[:, :LANES] = other_ref[...]
        work[:, LANES:] = mine_ref[...]

    halves = size // LANES
    lane = lax.broadcasted_iota(jnp.int32, (8, LANES), 1)
    sub = lax.broadcasted_iota(jnp.int32, (8, LANES), 0)
    wide = (8, LANES)
    for begin in range(0, size, STEP):
        tiles = [
            [work[begin + 8 * t : begin + 8 * t + 8, LANES * h : LANES * (h + 1)] for h in range(halves)]
            for t in range(STEP // 8)
        ]
        hot = begin // LANES
        for j in range(0, STEP, GROUP):
            t0, r0 = j // 8, j % 8
            l0 = (begin + j) % LANES
            below = range(t0, STEP // 8)
            cols = [
                {t: jnp.broadcast_to(tiles[t][hot][:, l0 + q : l0 + q + 1], wide) for t in below}
                for q in range(GROUP)
            ]
            rows = [
                [jnp.broadcast_to(tiles[t0][h][r0 + q : r0 + q + 1], wide) for h in range(halves)]
                for q in range(GROUP)
            ]
            small = {
                (i, q): jnp.broadcast_to(cols[q][t0][r0 + i : r0 + i + 1], wide)
                for q in range(GROUP)
                for i in range(q, GROUP)
            }
            for q in range(GROUP):
                inv = lax.rsqrt(small[q, q])
                at = lane == l0 + q
                rows[q] = [v * inv for v in rows[q]]
                rows[q][hot] = jnp.where(at, inv, rows[q][hot])
                cols[q] = {t: v * inv for t, v in cols[q].items()}
                ell = {i: small[i, q] * inv for i in range(q + 1, GROUP)}
                for i in range(q + 1, GROUP):
                    for p in range(q + 1, i + 1):
                        small[i, p] = small[i, p] - ell[i] * ell[p]
                    rows[i][hot] = jnp.where(at, 0.0, rows[i][hot])
                    rows[i] = [v - ell[i] * u for v, u in zip(rows[i], rows[q])]
                    cols[i] = {t: v - cols[q][t] * ell[i] for t, v in cols[i].items()}
            cleared = jnp.logical_and(lane >= l0, lane < l0 + GROUP)
            for q in range(GROUP - 1):
                stale = jnp.logical_and(lane > l0 + q, lane < l0 + GROUP)
                rows[q][hot] = jnp.where(stale, 0.0, rows[q][hot])
            for t in below:
                fresh = []
                for h in range(halves):
                    value = tiles[t][h]
                    if h == hot:
                        value = jnp.where(cleared, 0.0, value)
                    for q in range(GROUP):
                        value = value - cols[q][t] * rows[q][h]
                    if t == t0:
                        value = jnp.where(sub < r0, tiles[t][h], value)
                        for q in range(GROUP):
                            value = jnp.where(sub == r0 + q, rows[q][h], value)
                    fresh.append(value)
                tiles[t] = fresh
        panel = jnp.concatenate([jnp.concatenate(t, axis=1) for t in tiles], axis=0)
        column = lax.broadcasted_iota(jnp.int32, (STEP, size), 1)
        line = lax.broadcasted_iota(jnp.int32, (STEP, size), 0) + begin
        upper = jnp.logical_and(column > line, column < begin + STEP)
        panel = jnp.where(upper, 0.0, panel)
        out_ref[begin : begin + STEP, :] = jnp.where(column < begin + STEP, panel, 0.0)
        if begin + STEP < size:
            base = (begin + STEP) // LANES * LANES
            ahead = jnp.where(column >= begin + STEP, panel, 0.0)[:, base:]
            update = contract(ahead, panel, ((0,), (0,)), HIGHEST)
            here = lax.broadcasted_iota(jnp.int32, (size - base, size), 1)
            old = jnp.where(jnp.logical_and(here >= begin, here < begin + STEP), 0.0, work[base:, :])
            work[base:, :] = old - update


def residual_kernel(n_col, blocks, scale, where_ref, *refs):
    pieces = refs[:n_col]
    matrix_ref, mine_ref, other_ref, inverse_ref = refs[n_col : n_col + 4]
    rows_ref, out_ref, window, result, cross, sems, out_sems = refs[n_col + 4 :]
    col, core, x = where_ref[0], where_ref[1], where_ref[2]
    order = piece_order(col, n_col)
    rows = pieces[0].shape[0] // 2
    long = rows * blocks
    copies = []
    for spot in range(n_col):
        start = pl.multiple_of(order[spot] * long, long)
        copy = pltpu.make_async_copy(
            matrix_ref.at[pl.ds(start, long)], window.at[spot], sems.at[spot]
        )
        copy.start()
        copies.append(copy)
    quarters, quarter = mine_ref.shape[0], mine_ref.shape[1]
    for hop in range(quarters):
        spot = lax.rem(x + quarters - hop, quarters)
        base = pl.multiple_of((core * quarters + spot) * quarter, quarter)
        cross[pl.ds(base, quarter)] = mine_ref[hop]
        base = pl.multiple_of(((1 - core) * quarters + spot) * quarter, quarter)
        cross[pl.ds(base, quarter)] = other_ref[hop]
    inverse = inverse_ref[...]
    size = inverse.shape[0]
    every = jnp.concatenate([cross[size * b : size * (b + 1)] for b in range(blocks)], axis=1)
    top = contract(inverse, every, ((1,), (0,)), HIGHEST)
    weights = split(contract(inverse, top, ((0,), (0,)), HIGHEST))
    for block in range(blocks):
        rows_ref[pl.ds(block, size, stride=blocks), :] = (
            top[:, LANES * block : LANES * (block + 1)] * scale
        )
    outs = []
    for spot in range(n_col):
        panel = split(load_piece(pieces[spot]))
        fit = dot3(panel, weights, ((1,), (0,)))
        copies[spot].wait()
        for block in range(blocks):
            result[spot, pl.ds(block, rows, stride=blocks), :] = (
                window[spot, pl.ds(block, rows, stride=blocks), :]
                - fit[:, LANES * block : LANES * (block + 1)]
            )
        start = pl.multiple_of(order[spot] * long, long)
        out = pltpu.make_async_copy(
            result.at[spot], out_ref.at[pl.ds(start, long)], out_sems.at[spot]
        )
        out.start()
        outs.append(out)
    for out in outs:
        out.wait()


VMEM = pl.BlockSpec(memory_space=pltpu.VMEM)
ANY = pl.BlockSpec(memory_space=pl.ANY)
SMEM = pl.BlockSpec(memory_space=pltpu.SMEM)


def pick(value, index):
    return lax.dynamic_index_in_dim(value, index, 0, keepdims=False)


def row_perms(n_row):
    nx = ny = math.isqrt(n_row // 2)

    def rank(x, y, core):
        return (x % nx * ny + y % ny) * 2 + core

    def table(dx, dy, flip):
        return [
            (rank(x, y, core), rank(x + dx, y + dy, core ^ flip))
            for x in range(nx)
            for y in range(ny)
            for core in range(2)
        ]

    return (
        table(0, 0, 1),
        [table(s, 0, 0) for s in range(1, nx)],
        [table(0, s, 0) for s in range(1, ny)],
    )


def gather_sum(value, perms):
    got = [lax.ppermute(value, "row", perm) for perm in perms]
    return (value + got[1]) + (got[0] + got[2])


def sum_small(value, core, perms):
    swap, along_x, along_y = perms
    half = value.reshape(2, -1, LANES)
    mine = pick(half, core) + lax.ppermute(pick(half, 1 - core), "row", swap)
    mine = gather_sum(gather_sum(mine, along_x), along_y)
    return mine, lax.ppermute(mine, "row", swap)


def sum_large(value, core, x, perms):
    swap, along_x, along_y = perms
    nx = len(along_x) + 1
    half = value.reshape(2, nx, -1, LANES)
    mine = pick(half, core) + lax.ppermute(pick(half, 1 - core), "row", swap)
    got = [lax.ppermute(pick(mine, lax.rem(x + s + 1, nx)), "row", p) for s, p in enumerate(along_x)]
    part = (pick(mine, x) + got[1]) + (got[0] + got[2])
    part = gather_sum(part, along_y)
    mine = jnp.stack([part] + [lax.ppermute(part, "row", p) for p in along_x])
    return mine, lax.ppermute(mine, "row", swap)


def spread_panel(own, col, n_col):
    pieces = own.reshape(n_col, -1, LANES)
    got = [None]
    for s in range(1, n_col):
        pairs = [(0, s), (1, (1 + s) % n_col)]
        got.append(lax.ppermute(pick(pieces, lax.rem(col + s, n_col)), "col", pairs))
    first, second = pieces[0], pieces[1]
    for s in range(1, n_col):
        first = jnp.where(col == s, got[s], first)
        second = jnp.where(col == (1 + s) % n_col, got[s], second)
    piece = jnp.concatenate([first, second])
    up = [(c, (c + 1) % n_col) for c in range(n_col)]
    down = [(c, (c - 1) % n_col) for c in range(n_col)]
    ups, downs = [piece], [piece]
    for _ in range(n_col // 2 - 1):
        ups.append(lax.ppermute(ups[-1], "col", up))
        downs.append(lax.ppermute(downs[-1], "col", down))
    mid = piece.shape[0] // 2
    last = jnp.concatenate(
        [lax.ppermute(ups[-1][:mid], "col", up), lax.ppermute(downs[-1][mid:], "col", down)]
    )
    order = [piece]
    for u, d in zip(ups[1:], downs[1:]):
        order += [u, d]
    return order + [last]


def per_device(n_row, n_col, matrix):
    rows_here, blocks, _, width = matrix.shape
    flat = matrix.reshape(rows_here * blocks, width)
    col = lax.axis_index("col")
    row = lax.axis_index("row")
    perms = row_perms(n_row)
    nx = len(perms[1]) + 1
    core = lax.rem(row, 2)
    x = row // (n_row // nx)
    where = jnp.stack([col, core, x]).astype(jnp.int32)
    size = 2 * width
    pieces = spread_panel(matrix[:, 0, 0, :], col, n_col)
    depth = rows_here // n_col
    long = depth * blocks
    f32 = jnp.float32
    total = rows_here * size * (size + blocks * width)
    gram, cross = pl.pallas_call(
        functools.partial(products_kernel, n_col, blocks),
        out_shape=(
            jax.ShapeDtypeStruct((2, size, width), f32),
            jax.ShapeDtypeStruct((blocks, size, width), f32),
        ),
        in_specs=[SMEM] + [VMEM] * n_col + [ANY],
        out_specs=(VMEM, VMEM),
        scratch_shapes=[
            pltpu.VMEM((n_col, long, width), f32),
            pltpu.SemaphoreType.DMA((n_col,)),
        ],
        compiler_params=pltpu.CompilerParams(vmem_limit_bytes=40 << 20),
        cost_estimate=pl.CostEstimate(
            flops=6 * total, bytes_accessed=4 * rows_here * (size + blocks * width), transcendentals=0
        ),
        name="products",
    )(where, *pieces, flat)
    mine, other = sum_small(gram, core, perms)
    cross_mine, cross_other = sum_large(cross, core, x, perms)
    inverse = pl.pallas_call(
        factor_kernel,
        out_shape=jax.ShapeDtypeStruct((size, size), f32),
        in_specs=[SMEM, VMEM, VMEM],
        out_specs=VMEM,
        scratch_shapes=[pltpu.VMEM((size, size), f32)],
        compiler_params=pltpu.CompilerParams(vmem_limit_bytes=16 << 20),
        cost_estimate=pl.CostEstimate(
            flops=10 * size**3, bytes_accessed=8 * size * size, transcendentals=size
        ),
        name="factor",
    )(where, mine, other)
    scaled, residual = pl.pallas_call(
        functools.partial(residual_kernel, n_col, blocks, 1.0 / math.sqrt(rows_here * n_row)),
        out_shape=(
            jax.ShapeDtypeStruct((size * blocks, width), f32),
            jax.ShapeDtypeStruct((rows_here * blocks, width), f32),
        ),
        in_specs=[SMEM] + [VMEM] * n_col + [ANY, VMEM, VMEM, VMEM],
        out_specs=(VMEM, ANY),
        scratch_shapes=[
            pltpu.VMEM((n_col, long, width), f32),
            pltpu.VMEM((n_col, long, width), f32),
            pltpu.VMEM((size * blocks, width), f32),
            pltpu.SemaphoreType.DMA((n_col,)),
            pltpu.SemaphoreType.DMA((n_col,)),
        ],
        compiler_params=pltpu.CompilerParams(vmem_limit_bytes=48 << 20),
        cost_estimate=pl.CostEstimate(
            flops=6 * total, bytes_accessed=8 * rows_here * (size + blocks * width), transcendentals=0
        ),
        name="residual",
    )(where, *pieces, flat, cross_mine, cross_other, inverse)
    return (
        scaled.reshape(size, blocks, 1, width),
        residual.reshape(rows_here, blocks, 1, width),
    )


def solution(mesh):
    return jax.shard_map(
        functools.partial(per_device, mesh.shape["row"], mesh.shape["col"]),
        mesh=mesh,
        in_specs=(P("row", None, "col", None),),
        out_specs=(P(None, None, "col", None), P("row", None, "col", None)),
        check_vma=False,
    )
```

```python
import functools
import math

import jax
import jax.numpy as jnp
from jax import lax
from jax.experimental import pallas as pl
from jax.experimental.pallas import tpu as pltpu
from jax.sharding import PartitionSpec as P

LANES = 128
STEP = 32
GROUP = 4
SPAN = 64
HIGHEST = lax.Precision.HIGHEST


def split(value):
    high = value.astype(jnp.bfloat16)
    low = (value - high.astype(jnp.float32)).astype(jnp.bfloat16)
    return high, low


def contract(left, right, dims, precision=None):
    return lax.dot_general(
        left, right, (dims, ((), ())), precision=precision, preferred_element_type=jnp.float32
    )


def dot3(left, right, dims):
    (lh, ll), (rh, rl) = left, right
    return contract(lh, rh, dims) + (contract(lh, rl, dims) + contract(ll, rh, dims))


def dot4(left, right, dims):
    return dot3(left, right, dims) + contract(left[1], right[1], dims)


def sources(col, hop, n_col):
    if hop == 0 or 2 * hop == n_col:
        return [lax.rem(col + hop, n_col)]
    return [lax.rem(col + n_col - hop, n_col), lax.rem(col + hop, n_col)]


def load_piece(refs):
    if len(refs) == 1:
        half = refs[0].shape[0] // 2
        return jnp.concatenate([refs[0][:half], refs[0][half:]], axis=1)
    return jnp.concatenate([refs[0][...], refs[1][...]], axis=1)


def fetch(matrix_ref, window_ref, sem, chunk, long):
    start = pl.multiple_of(chunk * long, long)
    return pltpu.make_async_copy(matrix_ref.at[pl.ds(start, long)], window_ref, sem)


def load_blocks(window_ref, rows, blocks):
    return jnp.concatenate(
        [window_ref[pl.ds(block, rows, stride=blocks), :] for block in range(blocks)], axis=1
    )


FIRST = ((0,), (0,))


def gram_kernel(piece_ref, gram_ref):
    half = piece_ref.shape[0] // 2
    left, right = split(piece_ref[:half]), split(piece_ref[half:])
    gram_ref[0] = dot4(left, left, FIRST)
    gram_ref[1] = dot4(right, right, FIRST)
    gram_ref[2] = dot4(left, right, FIRST)


def collect_kernel(hop, n_col, blocks, shapes, where_ref, *refs):
    pieces = []
    for count in shapes:
        pieces.append(refs[:count])
        refs = refs[count:]
    matrix_ref, refs = refs[0], refs[1:]
    if hop:
        cross_in, refs = refs[0], refs[1:]
    cross_ref, window, sems = refs
    long = window.shape[1]
    rows = long // blocks
    copies = [
        fetch(matrix_ref, window.at[i], sems.at[i], chunk, long)
        for i, chunk in enumerate(sources(where_ref[0], hop, n_col))
    ]
    for copy in copies:
        copy.start()
    total = None
    for i, copy in enumerate(copies):
        panel = split(load_piece(pieces[i]))
        copy.wait()
        term = dot3(panel, split(load_blocks(window.at[i], rows, blocks)), FIRST)
        total = term if total is None else total + term
    for b in range(blocks):
        term = total[:, LANES * b : LANES * (b + 1)]
        cross_ref[b] = cross_in[b] + term if hop else term


def factor_kernel(begin, end, where_ref, *refs):
    if begin == 0:
        mine_ref, other_ref, work, parts = refs
        core = where_ref[1]
        count = mine_ref.shape[0]
        parts[pl.ds(pl.multiple_of(core * count, count), count)] = mine_ref[...]
        parts[pl.ds(pl.multiple_of((1 - core) * count, count), count)] = other_ref[...]
        work[:LANES, :LANES] = parts[:LANES]
        work[:LANES, LANES:] = parts[2 * LANES :]
        work[LANES:, :LANES] = jnp.zeros((LANES, LANES), jnp.float32)
        work[LANES:, LANES:] = parts[LANES : 2 * LANES]
    else:
        work_in, work = refs
        work[...] = work_in[...]
    size = work.shape[0]
    halves = size // LANES
    lane = lax.broadcasted_iota(jnp.int32, (8, LANES), 1)
    sub = lax.broadcasted_iota(jnp.int32, (8, LANES), 0)
    wide = (8, LANES)
    for begin in range(begin, end, STEP):
        tiles = [
            [work[begin + 8 * t : begin + 8 * t + 8, LANES * h : LANES * (h + 1)] for h in range(halves)]
            for t in range(STEP // 8)
        ]
        hot = begin // LANES
        for j in range(0, STEP, GROUP):
            t0, r0 = j // 8, j % 8
            l0 = (begin + j) % LANES
            below = range(t0, STEP // 8)
            cols = [
                {t: jnp.broadcast_to(tiles[t][hot][:, l0 + q : l0 + q + 1], wide) for t in below}
                for q in range(GROUP)
            ]
            rows = [
                [jnp.broadcast_to(tiles[t0][h][r0 + q : r0 + q + 1], wide) for h in range(halves)]
                for q in range(GROUP)
            ]
            small = {
                (i, q): jnp.broadcast_to(cols[q][t0][r0 + i : r0 + i + 1], wide)
                for q in range(GROUP)
                for i in range(q, GROUP)
            }
            for q in range(GROUP):
                inv = lax.rsqrt(small[q, q])
                at = lane == l0 + q
                rows[q] = [v * inv for v in rows[q]]
                rows[q][hot] = jnp.where(at, inv, rows[q][hot])
                cols[q] = {t: v * inv for t, v in cols[q].items()}
                ell = {i: small[i, q] * inv for i in range(q + 1, GROUP)}
                for i in range(q + 1, GROUP):
                    for p in range(q + 1, i + 1):
                        small[i, p] = small[i, p] - ell[i] * ell[p]
                    rows[i][hot] = jnp.where(at, 0.0, rows[i][hot])
                    rows[i] = [v - ell[i] * u for v, u in zip(rows[i], rows[q])]
                    cols[i] = {t: v - cols[q][t] * ell[i] for t, v in cols[i].items()}
            cleared = jnp.logical_and(lane >= l0, lane < l0 + GROUP)
            for q in range(GROUP - 1):
                stale = jnp.logical_and(lane > l0 + q, lane < l0 + GROUP)
                rows[q][hot] = jnp.where(stale, 0.0, rows[q][hot])
            for t in below:
                fresh = []
                for h in range(halves):
                    value = tiles[t][h]
                    if h == hot:
                        value = jnp.where(cleared, 0.0, value)
                    for q in range(GROUP):
                        value = value - cols[q][t] * rows[q][h]
                    if t == t0:
                        value = jnp.where(sub < r0, tiles[t][h], value)
                        for q in range(GROUP):
                            value = jnp.where(sub == r0 + q, rows[q][h], value)
                    fresh.append(value)
                tiles[t] = fresh
        panel = jnp.concatenate([jnp.concatenate(t, axis=1) for t in tiles], axis=0)
        column = lax.broadcasted_iota(jnp.int32, (STEP, size), 1)
        line = lax.broadcasted_iota(jnp.int32, (STEP, size), 0) + begin
        upper = jnp.logical_and(column > line, column < begin + STEP)
        panel = jnp.where(upper, 0.0, panel)
        if begin + STEP < size:
            base = (begin + STEP) // LANES * LANES
            ahead = jnp.where(column >= begin + STEP, panel, 0.0)[:, base:]
            update = contract(ahead, panel, ((0,), (0,)), HIGHEST)
            here = lax.broadcasted_iota(jnp.int32, (size - base, size), 1)
            old = jnp.where(jnp.logical_and(here >= begin, here < begin + STEP), 0.0, work[base:, :])
            work[base:, :] = old - update
        work[begin : begin + STEP, :] = jnp.where(column < begin + STEP, panel, 0.0)


def residual_kernel(n_col, blocks, scale, shapes, where_ref, *refs):
    pieces = []
    for count in shapes:
        pieces.append(refs[:count])
        refs = refs[count:]
    matrix_ref, mine_ref, other_ref, inverse_ref = refs[:4]
    rows_ref, out_ref, window, result, cross, sems, out_sems = refs[4:]
    col, core, x = where_ref[0], where_ref[1], where_ref[2]
    order = sum([sources(col, hop, n_col) for hop in range(n_col // 2 + 1)], [])
    long = window.shape[1]
    rows = long // blocks
    copies = [
        fetch(matrix_ref, window.at[i], sems.at[i], chunk, long) for i, chunk in enumerate(order)
    ]
    for copy in copies:
        copy.start()
    quarters, quarter = mine_ref.shape[0], mine_ref.shape[1]
    for hop in range(quarters):
        spot = lax.rem(x + quarters - hop, quarters)
        base = pl.multiple_of((core * quarters + spot) * quarter, quarter)
        cross[pl.ds(base, quarter)] = mine_ref[hop]
        base = pl.multiple_of(((1 - core) * quarters + spot) * quarter, quarter)
        cross[pl.ds(base, quarter)] = other_ref[hop]
    inverse = inverse_ref[...]
    size = inverse.shape[0]
    every = jnp.concatenate([cross[size * b : size * (b + 1)] for b in range(blocks)], axis=1)
    top = contract(inverse, every, ((1,), (0,)), HIGHEST)
    weights = split(contract(inverse, top, FIRST, HIGHEST))
    for block in range(blocks):
        rows_ref[pl.ds(block, size, stride=blocks), :] = (
            top[:, LANES * block : LANES * (block + 1)] * scale
        )
    outs = []
    for i, copy in enumerate(copies):
        fit = dot3(split(load_piece(pieces[i])), weights, ((1,), (0,)))
        copy.wait()
        for block in range(blocks):
            result[i, pl.ds(block, rows, stride=blocks), :] = (
                window[i, pl.ds(block, rows, stride=blocks), :]
                - fit[:, LANES * block : LANES * (block + 1)]
            )
        start = pl.multiple_of(order[i] * long, long)
        out = pltpu.make_async_copy(
            result.at[i], out_ref.at[pl.ds(start, long)], out_sems.at[i]
        )
        out.start()
        outs.append(out)
    for out in outs:
        out.wait()


VMEM = pl.BlockSpec(memory_space=pltpu.VMEM)
ANY = pl.BlockSpec(memory_space=pl.ANY)
HBM = pl.BlockSpec(memory_space=pltpu.HBM)
SMEM = pl.BlockSpec(memory_space=pltpu.SMEM)


def pick(value, index):
    return lax.dynamic_index_in_dim(value, index, 0, keepdims=False)


def row_perms(n_row):
    nx = ny = math.isqrt(n_row // 2)

    def rank(x, y, core):
        return (x % nx * ny + y % ny) * 2 + core

    def table(dx, dy, flip):
        return [
            (rank(x, y, core), rank(x + dx, y + dy, core ^ flip))
            for x in range(nx)
            for y in range(ny)
            for core in range(2)
        ]

    return (
        table(0, 0, 1),
        [table(s, 0, 0) for s in range(1, nx)],
        [table(0, s, 0) for s in range(1, ny)],
    )


def send(value, perms):
    return [lax.ppermute(value, "row", perm) for perm in perms]


def total(value, got):
    return (value + got[1]) + (got[0] + got[2])


def hand_out(own, col, n_col):
    pieces = own.reshape(n_col, -1, LANES)
    first, second = pieces[0], pieces[1]
    for s in range(1, n_col):
        pairs = [(0, s), (1, (1 + s) % n_col)]
        got = lax.ppermute(pick(pieces, lax.rem(col + s, n_col)), "col", pairs)
        first = jnp.where(col == s, got, first)
        second = jnp.where(col == (1 + s) % n_col, got, second)
    return jnp.concatenate([first, second])


def after(value, *done):
    return lax.optimization_barrier((value, *done))[0]


def estimate(flops, moved):
    return pl.CostEstimate(flops=flops, bytes_accessed=moved, transcendentals=0)


def per_device(n_row, n_col, matrix):
    rows_here, blocks, _, width = matrix.shape
    flat = matrix.reshape(rows_here * blocks, width)
    col = lax.axis_index("col")
    row = lax.axis_index("row")
    perms = row_perms(n_row)
    nx = len(perms[1]) + 1
    core = lax.rem(row, 2)
    x = row // (n_row // nx)
    where = jnp.stack([col, core, x]).astype(jnp.int32)
    size = 2 * width
    rows = rows_here // n_col
    long = rows * blocks
    f32 = jnp.float32
    shape = jax.ShapeDtypeStruct
    flat = pltpu.with_memory_space_constraint(flat, pltpu.HBM)
    cross_shape = shape((blocks, size, width), f32)

    def collect(hop, pieces, *state):
        shapes = [len(p) for p in pieces]
        return pl.pallas_call(
            functools.partial(collect_kernel, hop, n_col, blocks, shapes),
            out_shape=cross_shape,
            in_specs=[SMEM] + [VMEM] * sum(shapes) + [HBM] + [VMEM] * len(state),
            out_specs=VMEM,
            scratch_shapes=[
                pltpu.VMEM((len(pieces), long, width), f32),
                pltpu.SemaphoreType.DMA((len(pieces),)),
            ],
            compiler_params=pltpu.CompilerParams(vmem_limit_bytes=12 << 20),
            cost_estimate=estimate(
                6 * len(pieces) * rows * size * blocks * width,
                4 * len(pieces) * long * width,
            ),
            name="collect",
        )(where, *sum(pieces, []), flat, *state)

    def factor(begin, *given):
        start = begin == 0
        return pl.pallas_call(
            functools.partial(factor_kernel, begin, begin + SPAN),
            out_shape=shape((size, size), f32),
            in_specs=[SMEM] + [VMEM] * len(given),
            out_specs=VMEM,
            scratch_shapes=[pltpu.VMEM((3 * width, width), f32)] if start else [],
            compiler_params=pltpu.CompilerParams(vmem_limit_bytes=8 << 20),
            cost_estimate=estimate(64 * size**3 * SPAN // size, 8 * size * size),
            name="factor",
        )(where, *given)

    up = [(c, (c + 1) % n_col) for c in range(n_col)]
    down = [(c, (c - 1) % n_col) for c in range(n_col)]
    flips = [[(c, c ^ bit) for c in range(n_col)] for bit in (1, 2, 4)]
    swap, along_x, along_y = perms
    piece = hand_out(matrix[:, 0, 0, :], col, n_col)
    gram = pl.pallas_call(
        gram_kernel,
        out_shape=shape((3, width, width), f32),
        in_specs=[VMEM],
        out_specs=VMEM,
        compiler_params=pltpu.CompilerParams(vmem_limit_bytes=8 << 20),
        cost_estimate=estimate(8 * rows * size * width, 4 * rows * size),
        name="gram",
    )(piece)
    every = [[piece]]

    left, right = lax.ppermute(piece, "col", up), lax.ppermute(piece, "col", down)
    pair = gram.reshape(2, -1, width)
    mine = pick(pair, core) + lax.ppermute(pick(pair, 1 - core), "row", swap)
    got = send(mine, along_x)
    cross = collect(0, [[piece]])
    left, right, cross = lax.optimization_barrier((left, right, cross))
    every += [[left], [right]]

    left, right = lax.ppermute(left, "col", up), lax.ppermute(right, "col", down)
    mine = total(mine, got)
    got = send(mine, along_y)
    cross = collect(1, every[1:3], cross)
    left, right, cross, mine = lax.optimization_barrier((left, right, cross, mine))
    every += [[left], [right]]

    left, right = lax.ppermute(left, "col", up), lax.ppermute(right, "col", down)
    mine = total(mine, got)
    got = lax.ppermute(mine, "col", flips[0])
    cross = collect(2, every[3:5], cross)
    left, right, cross, mine = lax.optimization_barrier((left, right, cross, mine))
    every += [[left], [right]]

    last = [
        lax.ppermute(left[:rows], "col", up),
        lax.ppermute(right[rows:], "col", down),
    ]
    mine = mine + got
    got = lax.ppermute(mine, "col", flips[1])
    cross = collect(3, every[5:7], cross)
    *last, cross, mine, got = lax.optimization_barrier((*last, cross, mine, got))
    every += [last]

    cross = collect(4, [last], cross)
    whole = cross.reshape(2, nx, -1, width)
    other = lax.ppermute(pick(whole, 1 - core), "row", swap)
    mine = mine + got
    got = lax.ppermute(mine, "col", flips[2])
    part = after(pick(whole, core) + other, mine)
    took = [
        lax.ppermute(pick(part, lax.rem(x + s + 1, nx)), "row", p) for s, p in enumerate(along_x)
    ]
    mine = mine + got
    other = lax.ppermute(mine, "row", swap)
    work = factor(0, mine, other)
    part = after(total(pick(part, x), took), work)
    took = send(part, along_y)
    work = factor(SPAN, work)
    part = after(total(part, took), work)
    took = send(part, along_x)
    work = factor(2 * SPAN, work)
    cross_mine = after(jnp.stack([part, *took]), work)
    cross_other = lax.ppermute(cross_mine, "row", swap)
    work = factor(3 * SPAN, work)
    shapes = [len(p) for p in every]
    scaled, residual = pl.pallas_call(
        functools.partial(
            residual_kernel, n_col, blocks, 1.0 / math.sqrt(rows_here * n_row), shapes
        ),
        out_shape=(
            shape((size * blocks, width), f32),
            shape((rows_here * blocks, width), f32),
        ),
        in_specs=[SMEM] + [VMEM] * sum(shapes) + [HBM, VMEM, VMEM, VMEM],
        out_specs=(VMEM, HBM),
        scratch_shapes=[
            pltpu.VMEM((n_col, long, width), f32),
            pltpu.VMEM((n_col, long, width), f32),
            pltpu.VMEM((size * blocks, width), f32),
            pltpu.SemaphoreType.DMA((n_col,)),
            pltpu.SemaphoreType.DMA((n_col,)),
        ],
        compiler_params=pltpu.CompilerParams(vmem_limit_bytes=28 << 20),
        cost_estimate=estimate(
            6 * rows_here * size * blocks * width, 4 * rows_here * (size + 2 * blocks * width)
        ),
        name="residual",
    )(where, *sum(every, []), flat, cross_mine, cross_other, work)
    return (
        scaled.reshape(size, blocks, 1, width),
        residual.reshape(rows_here, blocks, 1, width),
    )


def solution(mesh):
    return jax.shard_map(
        functools.partial(per_device, mesh.shape["row"], mesh.shape["col"]),
        mesh=mesh,
        in_specs=(P("row", None, "col", None),),
        out_specs=(P(None, None, "col", None), P("row", None, "col", None)),
        check_vma=False,
    )
```

```python
import functools
import math

import jax
import jax.numpy as jnp
from jax import lax
from jax.experimental import pallas as pl
from jax.experimental.pallas import tpu as pltpu
from jax.sharding import PartitionSpec as P

LANES = 128
STEP = 32
GROUP = 4
SPAN = 64
HIGHEST = lax.Precision.HIGHEST


def split(value):
    high = value.astype(jnp.bfloat16)
    low = (value - high.astype(jnp.float32)).astype(jnp.bfloat16)
    return high, low


def contract(left, right, dims, precision=None):
    return lax.dot_general(
        left, right, (dims, ((), ())), precision=precision, preferred_element_type=jnp.float32
    )


def dot3(left, right, dims):
    (lh, ll), (rh, rl) = left, right
    return contract(lh, rh, dims) + (contract(lh, rl, dims) + contract(ll, rh, dims))


def dot4(left, right, dims):
    return dot3(left, right, dims) + contract(left[1], right[1], dims)


def sources(col, hop, n_col):
    if hop == 0 or 2 * hop == n_col:
        return [lax.rem(col + hop, n_col)]
    return [lax.rem(col + n_col - hop, n_col), lax.rem(col + hop, n_col)]


def load_piece(refs):
    if len(refs) == 1:
        half = refs[0].shape[0] // 2
        return jnp.concatenate([refs[0][:half], refs[0][half:]], axis=1)
    return jnp.concatenate([refs[0][...], refs[1][...]], axis=1)


def fetch(matrix_ref, window_ref, sem, chunk, long):
    start = pl.multiple_of(chunk * long, long)
    return pltpu.make_async_copy(matrix_ref.at[pl.ds(start, long)], window_ref, sem)


def load_blocks(window_ref, rows, blocks):
    return jnp.concatenate(
        [window_ref[pl.ds(block, rows, stride=blocks), :] for block in range(blocks)], axis=1
    )


FIRST = ((0,), (0,))


def gram_kernel(piece_ref, gram_ref):
    half = piece_ref.shape[0] // 2
    left, right = split(piece_ref[:half]), split(piece_ref[half:])
    gram_ref[0] = dot4(left, left, FIRST)
    gram_ref[1] = dot4(right, right, FIRST)
    gram_ref[2] = dot4(left, right, FIRST)


def stage_kernel(blocks, matrix_ref, high_ref, low_ref, window, sems):
    chunks, long = window.shape[0], window.shape[1]
    rows = long // blocks
    copies = [fetch(matrix_ref, window.at[i], sems.at[i], i, long) for i in range(chunks)]
    for copy in copies:
        copy.start()
    for i, copy in enumerate(copies):
        copy.wait()
        for b in range(blocks):
            high, low = split(window[i, pl.ds(b, rows, stride=blocks), :])
            high_ref[i, :, LANES * b : LANES * (b + 1)] = high
            low_ref[i, :, LANES * b : LANES * (b + 1)] = low


def collect_kernel(hop, n_col, shapes, where_ref, *refs):
    pieces = []
    for count in shapes:
        pieces.append(refs[:count])
        refs = refs[count:]
    high_ref, low_ref, cross_ref = refs[0], refs[1], refs[-1]
    total = None
    for i, chunk in enumerate(sources(where_ref[0], hop, n_col)):
        panel = split(load_piece(pieces[i]))
        term = dot3(panel, (high_ref[chunk], low_ref[chunk]), FIRST)
        total = term if total is None else total + term
    for b in range(cross_ref.shape[0]):
        term = total[:, LANES * b : LANES * (b + 1)]
        cross_ref[b] = refs[2][b] + term if hop else term


def factor_kernel(begin, end, where_ref, *refs):
    if begin == 0:
        mine_ref, other_ref, work, parts = refs
        core = where_ref[1]
        count = mine_ref.shape[0]
        parts[pl.ds(pl.multiple_of(core * count, count), count)] = mine_ref[...]
        parts[pl.ds(pl.multiple_of((1 - core) * count, count), count)] = other_ref[...]
        work[:LANES, :LANES] = parts[:LANES]
        work[:LANES, LANES:] = parts[2 * LANES :]
        work[LANES:, :LANES] = jnp.zeros((LANES, LANES), jnp.float32)
        work[LANES:, LANES:] = parts[LANES : 2 * LANES]
    else:
        work_in, work = refs
        work[...] = work_in[...]
    size = work.shape[0]
    halves = size // LANES
    lane = lax.broadcasted_iota(jnp.int32, (8, LANES), 1)
    sub = lax.broadcasted_iota(jnp.int32, (8, LANES), 0)
    wide = (8, LANES)
    for begin in range(begin, end, STEP):
        tiles = [
            [work[begin + 8 * t : begin + 8 * t + 8, LANES * h : LANES * (h + 1)] for h in range(halves)]
            for t in range(STEP // 8)
        ]
        hot = begin // LANES
        for j in range(0, STEP, GROUP):
            t0, r0 = j // 8, j % 8
            l0 = (begin + j) % LANES
            below = range(t0, STEP // 8)
            cols = [
                {t: jnp.broadcast_to(tiles[t][hot][:, l0 + q : l0 + q + 1], wide) for t in below}
                for q in range(GROUP)
            ]
            rows = [
                [jnp.broadcast_to(tiles[t0][h][r0 + q : r0 + q + 1], wide) for h in range(halves)]
                for q in range(GROUP)
            ]
            small = {
                (i, q): jnp.broadcast_to(cols[q][t0][r0 + i : r0 + i + 1], wide)
                for q in range(GROUP)
                for i in range(q, GROUP)
            }
            for q in range(GROUP):
                inv = lax.rsqrt(small[q, q])
                at = lane == l0 + q
                rows[q] = [v * inv for v in rows[q]]
                rows[q][hot] = jnp.where(at, inv, rows[q][hot])
                cols[q] = {t: v * inv for t, v in cols[q].items()}
                ell = {i: small[i, q] * inv for i in range(q + 1, GROUP)}
                for i in range(q + 1, GROUP):
                    for p in range(q + 1, i + 1):
                        small[i, p] = small[i, p] - ell[i] * ell[p]
                    rows[i][hot] = jnp.where(at, 0.0, rows[i][hot])
                    rows[i] = [v - ell[i] * u for v, u in zip(rows[i], rows[q])]
                    cols[i] = {t: v - cols[q][t] * ell[i] for t, v in cols[i].items()}
            cleared = jnp.logical_and(lane >= l0, lane < l0 + GROUP)
            for q in range(GROUP - 1):
                stale = jnp.logical_and(lane > l0 + q, lane < l0 + GROUP)
                rows[q][hot] = jnp.where(stale, 0.0, rows[q][hot])
            for t in below:
                fresh = []
                for h in range(halves):
                    value = tiles[t][h]
                    if h == hot:
                        value = jnp.where(cleared, 0.0, value)
                    for q in range(GROUP):
                        value = value - cols[q][t] * rows[q][h]
                    if t == t0:
                        value = jnp.where(sub < r0, tiles[t][h], value)
                        for q in range(GROUP):
                            value = jnp.where(sub == r0 + q, rows[q][h], value)
                    fresh.append(value)
                tiles[t] = fresh
        panel = jnp.concatenate([jnp.concatenate(t, axis=1) for t in tiles], axis=0)
        column = lax.broadcasted_iota(jnp.int32, (STEP, size), 1)
        line = lax.broadcasted_iota(jnp.int32, (STEP, size), 0) + begin
        upper = jnp.logical_and(column > line, column < begin + STEP)
        panel = jnp.where(upper, 0.0, panel)
        if begin + STEP < size:
            base = (begin + STEP) // LANES * LANES
            ahead = jnp.where(column >= begin + STEP, panel, 0.0)[:, base:]
            update = contract(ahead, panel, ((0,), (0,)), HIGHEST)
            here = lax.broadcasted_iota(jnp.int32, (size - base, size), 1)
            old = jnp.where(jnp.logical_and(here >= begin, here < begin + STEP), 0.0, work[base:, :])
            work[base:, :] = old - update
        work[begin : begin + STEP, :] = jnp.where(column < begin + STEP, panel, 0.0)


def residual_kernel(n_col, blocks, scale, shapes, where_ref, *refs):
    pieces = []
    for count in shapes:
        pieces.append(refs[:count])
        refs = refs[count:]
    matrix_ref, mine_ref, other_ref, inverse_ref = refs[:4]
    rows_ref, out_ref, window, result, cross, high, low, sems, out_sems = refs[4:]
    col, core, x = where_ref[0], where_ref[1], where_ref[2]
    chunks, long = window.shape[0], window.shape[1]
    rows = long // blocks
    for i in range(chunks):
        fetch(matrix_ref, window.at[i], sems.at[i], i, long).start()
    order = sum([sources(col, hop, n_col) for hop in range(n_col // 2 + 1)], [])
    for piece, chunk in zip(pieces, order):
        high[chunk], low[chunk] = split(load_piece(piece))
    quarters, quarter = mine_ref.shape[0], mine_ref.shape[1]
    for hop in range(quarters):
        spot = lax.rem(x + quarters - hop, quarters)
        base = pl.multiple_of((core * quarters + spot) * quarter, quarter)
        cross[pl.ds(base, quarter)] = mine_ref[hop]
        base = pl.multiple_of(((1 - core) * quarters + spot) * quarter, quarter)
        cross[pl.ds(base, quarter)] = other_ref[hop]
    inverse = inverse_ref[...]
    size = inverse.shape[0]
    every = jnp.concatenate([cross[size * b : size * (b + 1)] for b in range(blocks)], axis=1)
    top = contract(inverse, every, ((1,), (0,)), HIGHEST)
    weights = split(contract(inverse, top, FIRST, HIGHEST))
    for block in range(blocks):
        rows_ref[pl.ds(block, size, stride=blocks), :] = (
            top[:, LANES * block : LANES * (block + 1)] * scale
        )
    high_weights, low_weights = weights

    def write(i):
        start = pl.multiple_of(i * long, long)
        return pltpu.make_async_copy(
            result.at[i], out_ref.at[pl.ds(start, long)], out_sems.at[i]
        )

    def step(i, carry):
        fit = dot3((high[i], low[i]), (high_weights, low_weights), ((1,), (0,)))
        fetch(matrix_ref, window.at[i], sems.at[i], i, long).wait()
        for block in range(blocks):
            result[i, pl.ds(block, rows, stride=blocks), :] = (
                window[i, pl.ds(block, rows, stride=blocks), :]
                - fit[:, LANES * block : LANES * (block + 1)]
            )
        write(i).start()
        return carry

    lax.fori_loop(0, chunks, step, 0)
    for i in range(chunks):
        write(i).wait()


VMEM = pl.BlockSpec(memory_space=pltpu.VMEM)
ANY = pl.BlockSpec(memory_space=pl.ANY)
HBM = pl.BlockSpec(memory_space=pltpu.HBM)
SMEM = pl.BlockSpec(memory_space=pltpu.SMEM)


def pick(value, index):
    return lax.dynamic_index_in_dim(value, index, 0, keepdims=False)


def row_perms(n_row):
    nx = ny = math.isqrt(n_row // 2)

    def rank(x, y, core):
        return (x % nx * ny + y % ny) * 2 + core

    def table(dx, dy, flip):
        return [
            (rank(x, y, core), rank(x + dx, y + dy, core ^ flip))
            for x in range(nx)
            for y in range(ny)
            for core in range(2)
        ]

    return (
        table(0, 0, 1),
        [table(s, 0, 0) for s in range(1, nx)],
        [table(0, s, 0) for s in range(1, ny)],
    )


def send(value, perms):
    return [lax.ppermute(value, "row", perm) for perm in perms]


def total(value, got):
    return (value + got[1]) + (got[0] + got[2])


def hand_out(own, spots, hits, n_col):
    pieces = own.reshape(n_col, -1, LANES)
    first, second = pieces[0], pieces[1]
    for s in range(1, n_col):
        pairs = [(0, s), (1, (1 + s) % n_col)]
        got = lax.ppermute(pick(pieces, spots[s]), "col", pairs)
        first = jnp.where(hits[s], got, first)
        second = jnp.where(hits[(1 + s) % n_col], got, second)
    return jnp.concatenate([first, second])


def after(value, *done):
    return lax.optimization_barrier((value, *done))[0]


def estimate(flops, moved):
    return pl.CostEstimate(flops=flops, bytes_accessed=moved, transcendentals=0)


def per_device(n_row, n_col, matrix):
    rows_here, blocks, _, width = matrix.shape
    col = lax.axis_index("col")
    row = lax.axis_index("row")
    perms = row_perms(n_row)
    nx = len(perms[1]) + 1
    core = lax.rem(row, 2)
    x = row // (n_row // nx)
    where = jnp.stack([col, core, x]).astype(jnp.int32)
    unsigned = jnp.uint32
    spots = [lax.rem(col + s, n_col).astype(unsigned) for s in range(n_col)]
    hits = [col == s for s in range(n_col)]
    steps = [lax.rem(x + s, nx).astype(unsigned) for s in range(nx)]
    this, that = core.astype(unsigned), (1 - core).astype(unsigned)
    matrix, where, spots, hits, steps, this, that = lax.optimization_barrier(
        (matrix, where, spots, hits, steps, this, that)
    )
    flat = matrix.reshape(rows_here * blocks, width)
    size = 2 * width
    rows = rows_here // n_col
    long = rows * blocks
    f32 = jnp.float32
    shape = jax.ShapeDtypeStruct
    flat = pltpu.with_memory_space_constraint(flat, pltpu.HBM)
    cross_shape = shape((blocks, size, width), f32)

    parts = (shape((n_col, rows, blocks * width), jnp.bfloat16),) * 2
    staged = pl.pallas_call(
        functools.partial(stage_kernel, blocks),
        out_shape=parts,
        in_specs=[HBM],
        out_specs=(VMEM, VMEM),
        scratch_shapes=[
            pltpu.VMEM((n_col, long, width), f32),
            pltpu.SemaphoreType.DMA((n_col,)),
        ],
        compiler_params=pltpu.CompilerParams(vmem_limit_bytes=12 << 20),
        cost_estimate=estimate(8 * rows_here * blocks * width, 8 * rows_here * blocks * width),
        name="stage",
    )(flat)

    def collect(hop, pieces, *state):
        shapes = [len(p) for p in pieces]
        return pl.pallas_call(
            functools.partial(collect_kernel, hop, n_col, shapes),
            out_shape=cross_shape,
            in_specs=[SMEM] + [VMEM] * (sum(shapes) + 2 + len(state)),
            out_specs=VMEM,
            compiler_params=pltpu.CompilerParams(vmem_limit_bytes=8 << 20),
            cost_estimate=estimate(
                6 * len(pieces) * rows * size * blocks * width,
                4 * len(pieces) * long * width,
            ),
            name="collect",
        )(where, *sum(pieces, []), *staged, *state)

    def factor(begin, *given):
        start = begin == 0
        return pl.pallas_call(
            functools.partial(factor_kernel, begin, begin + SPAN),
            out_shape=shape((size, size), f32),
            in_specs=[SMEM] + [VMEM] * len(given),
            out_specs=VMEM,
            scratch_shapes=[pltpu.VMEM((3 * width, width), f32)] if start else [],
            compiler_params=pltpu.CompilerParams(vmem_limit_bytes=8 << 20),
            cost_estimate=estimate(256 * size**3, 8 * size * size),
            name="factor",
        )(where, *given)

    up = [(c, (c + 1) % n_col) for c in range(n_col)]
    down = [(c, (c - 1) % n_col) for c in range(n_col)]
    flips = [[(c, c ^ bit) for c in range(n_col)] for bit in (4, 2, 1)]
    swap, along_x, along_y = perms
    piece = hand_out(matrix[:, 0, 0, :], spots, hits, n_col)
    piece, *staged = lax.optimization_barrier((piece, *staged))
    gram = pl.pallas_call(
        gram_kernel,
        out_shape=shape((3, width, width), f32),
        in_specs=[VMEM],
        out_specs=VMEM,
        compiler_params=pltpu.CompilerParams(vmem_limit_bytes=8 << 20),
        cost_estimate=estimate(8 * rows * size * width, 4 * rows * size),
        name="gram",
    )(piece)
    every = [[piece]]

    left, right = lax.ppermute(piece, "col", up), lax.ppermute(piece, "col", down)
    pair = gram.reshape(2, -1, width)
    mine = pick(pair, this) + lax.ppermute(pick(pair, that), "row", swap)
    got = send(mine, along_x)
    cross = collect(0, [[piece]])
    left, right, cross = lax.optimization_barrier((left, right, cross))
    every += [[left], [right]]

    left, right = lax.ppermute(left, "col", up), lax.ppermute(right, "col", down)
    mine = total(mine, got)
    got = send(mine, along_y)
    cross = collect(1, every[1:3], cross)
    left, right, cross, mine = lax.optimization_barrier((left, right, cross, mine))
    every += [[left], [right]]

    left, right = lax.ppermute(left, "col", up), lax.ppermute(right, "col", down)
    mine = total(mine, got)
    got = lax.ppermute(mine, "col", flips[0])
    cross = collect(2, every[3:5], cross)
    left, right, cross, mine = lax.optimization_barrier((left, right, cross, mine))
    every += [[left], [right]]

    last = [
        lax.ppermute(left[:rows], "col", up),
        lax.ppermute(right[rows:], "col", down),
    ]
    mine = mine + got
    got = lax.ppermute(mine, "col", flips[1])
    cross = collect(3, every[5:7], cross)
    *last, cross, mine, got = lax.optimization_barrier((*last, cross, mine, got))
    every += [last]

    mine = mine + got
    got = lax.ppermute(mine, "col", flips[2])
    cross = collect(4, [last], cross)
    whole = cross.reshape(2, nx, -1, width)
    part = pick(whole, this) + lax.ppermute(pick(whole, that), "row", swap)
    took = [
        lax.ppermute(pick(part, steps[s + 1]), "row", p) for s, p in enumerate(along_x)
    ]
    mine = mine + got
    other = lax.ppermute(mine, "row", swap)
    work = factor(0, mine, other)
    part = after(total(pick(part, steps[0]), took), work)
    took = send(part, along_y)
    work = factor(SPAN, work)
    part = after(total(part, took), work)
    took = send(part, along_x)
    work = factor(2 * SPAN, work)
    cross_mine = after(jnp.stack([part, *took]), work)
    cross_other = lax.ppermute(cross_mine, "row", swap)
    work = factor(3 * SPAN, work)
    shapes = [len(p) for p in every]
    scaled, residual = pl.pallas_call(
        functools.partial(
            residual_kernel, n_col, blocks, 1.0 / math.sqrt(rows_here * n_row), shapes
        ),
        out_shape=(
            shape((size * blocks, width), f32),
            shape((rows_here * blocks, width), f32),
        ),
        in_specs=[SMEM] + [VMEM] * sum(shapes) + [HBM, VMEM, VMEM, VMEM],
        out_specs=(VMEM, HBM),
        scratch_shapes=[
            pltpu.VMEM((n_col, long, width), f32),
            pltpu.VMEM((n_col, long, width), f32),
            pltpu.VMEM((size * blocks, width), f32),
            pltpu.VMEM((n_col, rows, size), jnp.bfloat16),
            pltpu.VMEM((n_col, rows, size), jnp.bfloat16),
            pltpu.SemaphoreType.DMA((n_col,)),
            pltpu.SemaphoreType.DMA((n_col,)),
        ],
        compiler_params=pltpu.CompilerParams(vmem_limit_bytes=28 << 20),
        cost_estimate=estimate(
            6 * rows_here * size * blocks * width, 4 * rows_here * (size + 2 * blocks * width)
        ),
        name="residual",
    )(where, *sum(every, []), flat, cross_mine, cross_other, work)
    return (
        scaled.reshape(size, blocks, 1, width),
        residual.reshape(rows_here, blocks, 1, width),
    )


def solution(mesh):
    return jax.shard_map(
        functools.partial(per_device, mesh.shape["row"], mesh.shape["col"]),
        mesh=mesh,
        in_specs=(P("row", None, "col", None),),
        out_specs=(P(None, None, "col", None), P("row", None, "col", None)),
        check_vma=False,
    )
```

```python
import functools
import math

import jax
import jax.numpy as jnp
from jax import lax
from jax.experimental import pallas as pl
from jax.experimental.pallas import tpu as pltpu
from jax.sharding import PartitionSpec as P

LANES = 128
STEP = 32
GROUP = 4
SPAN = 64
HIGHEST = lax.Precision.HIGHEST


def split(value):
    high = value.astype(jnp.bfloat16)
    low = (value - high.astype(jnp.float32)).astype(jnp.bfloat16)
    return high, low


def contract(left, right, dims, precision=None):
    return lax.dot_general(
        left, right, (dims, ((), ())), precision=precision, preferred_element_type=jnp.float32
    )


def dot3(left, right, dims):
    (lh, ll), (rh, rl) = left, right
    return contract(lh, rh, dims) + (contract(lh, rl, dims) + contract(ll, rh, dims))


def dot4(left, right, dims):
    return dot3(left, right, dims) + contract(left[1], right[1], dims)


def sources(col, hop, n_col):
    if hop == 0 or 2 * hop == n_col:
        return [lax.rem(col + hop, n_col)]
    return [lax.rem(col + n_col - hop, n_col), lax.rem(col + hop, n_col)]


def load_piece(refs):
    if len(refs) == 1:
        half = refs[0].shape[0] // 2
        return jnp.concatenate([refs[0][:half], refs[0][half:]], axis=1)
    return jnp.concatenate([refs[0][...], refs[1][...]], axis=1)


def fetch(matrix_ref, window_ref, sem, chunk, long):
    start = pl.multiple_of(chunk * long, long)
    return pltpu.make_async_copy(matrix_ref.at[pl.ds(start, long)], window_ref, sem)


def load_blocks(window_ref, rows, blocks):
    return jnp.concatenate(
        [window_ref[pl.ds(block, rows, stride=blocks), :] for block in range(blocks)], axis=1
    )


FIRST = ((0,), (0,))


def gram_kernel(piece_ref, gram_ref):
    half = piece_ref.shape[0] // 2
    left, right = split(piece_ref[:half]), split(piece_ref[half:])
    gram_ref[0] = dot4(left, left, FIRST)
    gram_ref[1] = dot4(right, right, FIRST)
    gram_ref[2] = dot4(left, right, FIRST)


def stage_kernel(blocks, matrix_ref, high_ref, low_ref, window, sems):
    chunks, long = window.shape[0], window.shape[1]
    rows = long // blocks
    copies = [fetch(matrix_ref, window.at[i], sems.at[i], i, long) for i in range(chunks)]
    for copy in copies:
        copy.start()
    for i, copy in enumerate(copies):
        copy.wait()
        for b in range(blocks):
            high, low = split(window[i, pl.ds(b, rows, stride=blocks), :])
            high_ref[i, :, LANES * b : LANES * (b + 1)] = high
            low_ref[i, :, LANES * b : LANES * (b + 1)] = low


def collect_kernel(hop, n_col, shapes, where_ref, *refs):
    pieces = []
    for count in shapes:
        pieces.append(refs[:count])
        refs = refs[count:]
    high_ref, low_ref, cross_ref = refs[0], refs[1], refs[-1]
    total = None
    for i, chunk in enumerate(sources(where_ref[0], hop, n_col)):
        panel = split(load_piece(pieces[i]))
        term = dot3(panel, (high_ref[chunk], low_ref[chunk]), FIRST)
        total = term if total is None else total + term
    for b in range(cross_ref.shape[0]):
        term = total[:, LANES * b : LANES * (b + 1)]
        cross_ref[b] = refs[2][b] + term if hop else term


def factor_kernel(begin, end, where_ref, *refs):
    if begin == 0:
        mine_ref, other_ref, work, parts = refs
        core, x = where_ref[1], where_ref[2]
        quarters, count = mine_ref.shape[0], mine_ref.shape[1]
        for hop in range(quarters):
            spot = lax.rem(x + quarters - hop, quarters)
            for side, ref in ((core, mine_ref), (1 - core, other_ref)):
                base = pl.multiple_of((side * quarters + spot) * count, count)
                parts[pl.ds(base, count)] = ref[hop]
        work[:LANES, :LANES] = parts[:LANES]
        work[:LANES, LANES:] = parts[2 * LANES :]
        work[LANES:, :LANES] = jnp.zeros((LANES, LANES), jnp.float32)
        work[LANES:, LANES:] = parts[LANES : 2 * LANES]
    else:
        work_in, work = refs
        work[...] = work_in[...]
    size = work.shape[0]
    halves = size // LANES
    lane = lax.broadcasted_iota(jnp.int32, (8, LANES), 1)
    sub = lax.broadcasted_iota(jnp.int32, (8, LANES), 0)
    wide = (8, LANES)
    for begin in range(begin, end, STEP):
        tiles = [
            [work[begin + 8 * t : begin + 8 * t + 8, LANES * h : LANES * (h + 1)] for h in range(halves)]
            for t in range(STEP // 8)
        ]
        hot = begin // LANES
        for j in range(0, STEP, GROUP):
            t0, r0 = j // 8, j % 8
            l0 = (begin + j) % LANES
            below = range(t0, STEP // 8)
            cols = [
                {t: jnp.broadcast_to(tiles[t][hot][:, l0 + q : l0 + q + 1], wide) for t in below}
                for q in range(GROUP)
            ]
            rows = [
                [jnp.broadcast_to(tiles[t0][h][r0 + q : r0 + q + 1], wide) for h in range(halves)]
                for q in range(GROUP)
            ]
            small = {
                (i, q): jnp.broadcast_to(cols[q][t0][r0 + i : r0 + i + 1], wide)
                for q in range(GROUP)
                for i in range(q, GROUP)
            }
            for q in range(GROUP):
                inv = lax.rsqrt(small[q, q])
                at = lane == l0 + q
                rows[q] = [v * inv for v in rows[q]]
                rows[q][hot] = jnp.where(at, inv, rows[q][hot])
                cols[q] = {t: v * inv for t, v in cols[q].items()}
                ell = {i: small[i, q] * inv for i in range(q + 1, GROUP)}
                for i in range(q + 1, GROUP):
                    for p in range(q + 1, i + 1):
                        small[i, p] = small[i, p] - ell[i] * ell[p]
                    rows[i][hot] = jnp.where(at, 0.0, rows[i][hot])
                    rows[i] = [v - ell[i] * u for v, u in zip(rows[i], rows[q])]
                    cols[i] = {t: v - cols[q][t] * ell[i] for t, v in cols[i].items()}
            cleared = jnp.logical_and(lane >= l0, lane < l0 + GROUP)
            for q in range(GROUP - 1):
                stale = jnp.logical_and(lane > l0 + q, lane < l0 + GROUP)
                rows[q][hot] = jnp.where(stale, 0.0, rows[q][hot])
            for t in below:
                fresh = []
                for h in range(halves):
                    value = tiles[t][h]
                    if h == hot:
                        value = jnp.where(cleared, 0.0, value)
                    for q in range(GROUP):
                        value = value - cols[q][t] * rows[q][h]
                    if t == t0:
                        value = jnp.where(sub < r0, tiles[t][h], value)
                        for q in range(GROUP):
                            value = jnp.where(sub == r0 + q, rows[q][h], value)
                    fresh.append(value)
                tiles[t] = fresh
        panel = jnp.concatenate([jnp.concatenate(t, axis=1) for t in tiles], axis=0)
        column = lax.broadcasted_iota(jnp.int32, (STEP, size), 1)
        line = lax.broadcasted_iota(jnp.int32, (STEP, size), 0) + begin
        upper = jnp.logical_and(column > line, column < begin + STEP)
        panel = jnp.where(upper, 0.0, panel)
        if begin + STEP < size:
            base = (begin + STEP) // LANES * LANES
            ahead = jnp.where(column >= begin + STEP, panel, 0.0)[:, base:]
            update = contract(ahead, panel, ((0,), (0,)), HIGHEST)
            here = lax.broadcasted_iota(jnp.int32, (size - base, size), 1)
            old = jnp.where(jnp.logical_and(here >= begin, here < begin + STEP), 0.0, work[base:, :])
            work[base:, :] = old - update
        work[begin : begin + STEP, :] = jnp.where(column < begin + STEP, panel, 0.0)


def residual_kernel(n_col, blocks, scale, shapes, where_ref, *refs):
    pieces = []
    for count in shapes:
        pieces.append(refs[:count])
        refs = refs[count:]
    matrix_ref, mine_ref, other_ref, inverse_ref = refs[:4]
    rows_ref, out_ref, window, result, cross, high, low, sems, out_sems = refs[4:]
    col, core = where_ref[0], where_ref[1]
    chunks, long = window.shape[0], window.shape[1]
    rows = long // blocks
    for i in range(chunks):
        fetch(matrix_ref, window.at[i], sems.at[i], i, long).start()
    order = sum([sources(col, hop, n_col) for hop in range(n_col // 2 + 1)], [])
    for piece, chunk in zip(pieces, order):
        high[chunk], low[chunk] = split(load_piece(piece))
    count = mine_ref.shape[0]
    cross[pl.ds(pl.multiple_of(core * count, count), count)] = mine_ref[...]
    cross[pl.ds(pl.multiple_of((1 - core) * count, count), count)] = other_ref[...]
    inverse = inverse_ref[...]
    size = inverse.shape[0]
    every = jnp.concatenate([cross[size * b : size * (b + 1)] for b in range(blocks)], axis=1)
    top = contract(inverse, every, ((1,), (0,)), HIGHEST)
    weights = split(contract(inverse, top, FIRST, HIGHEST))
    for block in range(blocks):
        rows_ref[pl.ds(block, size, stride=blocks), :] = (
            top[:, LANES * block : LANES * (block + 1)] * scale
        )
    high_weights, low_weights = weights

    def write(i):
        start = pl.multiple_of(i * long, long)
        return pltpu.make_async_copy(
            result.at[i], out_ref.at[pl.ds(start, long)], out_sems.at[i]
        )

    def step(i, carry):
        fit = dot3((high[i], low[i]), (high_weights, low_weights), ((1,), (0,)))
        fetch(matrix_ref, window.at[i], sems.at[i], i, long).wait()
        for block in range(blocks):
            result[i, pl.ds(block, rows, stride=blocks), :] = (
                window[i, pl.ds(block, rows, stride=blocks), :]
                - fit[:, LANES * block : LANES * (block + 1)]
            )
        write(i).start()
        return carry

    lax.fori_loop(0, chunks, step, 0)
    for i in range(chunks):
        write(i).wait()


VMEM = pl.BlockSpec(memory_space=pltpu.VMEM)
ANY = pl.BlockSpec(memory_space=pl.ANY)
HBM = pl.BlockSpec(memory_space=pltpu.HBM)
SMEM = pl.BlockSpec(memory_space=pltpu.SMEM)


def pick(value, index):
    return lax.dynamic_index_in_dim(value, index, 0, keepdims=False)


def row_perms(n_row):
    nx = ny = math.isqrt(n_row // 2)

    def rank(x, y, core):
        return (x % nx * ny + y % ny) * 2 + core

    def table(dx, dy, flip):
        return [
            (rank(x, y, core), rank(x + dx, y + dy, core ^ flip))
            for x in range(nx)
            for y in range(ny)
            for core in range(2)
        ]

    return (
        table(0, 0, 1),
        [table(s, 0, 0) for s in range(1, nx)],
        [table(0, s, 0) for s in range(1, ny)],
        [[rank(x, y, core) for x in range(nx) for y in range(ny)] for core in range(2)],
    )


def send(value, perms):
    return [lax.ppermute(value, "row", perm) for perm in perms]


def exchange(value, groups):
    return lax.all_to_all(value, "row", 0, 0, axis_index_groups=groups)


def total(value, got):
    return (value + got[1]) + (got[0] + got[2])


def hand_out(own, spots, hits, n_col):
    pieces = own.reshape(n_col, -1, LANES)
    first, second = pieces[0], pieces[1]
    for s in range(1, n_col):
        pairs = [(0, s), (1, (1 + s) % n_col)]
        got = lax.ppermute(pick(pieces, spots[s]), "col", pairs)
        first = jnp.where(hits[s], got, first)
        second = jnp.where(hits[(1 + s) % n_col], got, second)
    return jnp.concatenate([first, second])


def after(value, *done):
    return lax.optimization_barrier((value, *done))[0]


def estimate(flops, moved):
    return pl.CostEstimate(flops=flops, bytes_accessed=moved, transcendentals=0)


def per_device(n_row, n_col, matrix):
    rows_here, blocks, _, width = matrix.shape
    col = lax.axis_index("col")
    row = lax.axis_index("row")
    perms = row_perms(n_row)
    nx = len(perms[1]) + 1
    core = lax.rem(row, 2)
    x = row // (n_row // nx)
    where = jnp.stack([col, core, x]).astype(jnp.int32)
    unsigned = jnp.uint32
    spots = [lax.rem(col + s, n_col).astype(unsigned) for s in range(n_col)]
    hits = [col == s for s in range(n_col)]
    steps = [lax.rem(x + s, nx).astype(unsigned) for s in range(nx)]
    this, that = core.astype(unsigned), (1 - core).astype(unsigned)
    matrix, where, spots, hits, steps, this, that = lax.optimization_barrier(
        (matrix, where, spots, hits, steps, this, that)
    )
    flat = matrix.reshape(rows_here * blocks, width)
    size = 2 * width
    rows = rows_here // n_col
    long = rows * blocks
    f32 = jnp.float32
    shape = jax.ShapeDtypeStruct
    flat = pltpu.with_memory_space_constraint(flat, pltpu.HBM)
    cross_shape = shape((blocks, size, width), f32)

    parts = (shape((n_col, rows, blocks * width), jnp.bfloat16),) * 2
    staged = pl.pallas_call(
        functools.partial(stage_kernel, blocks),
        out_shape=parts,
        in_specs=[HBM],
        out_specs=(VMEM, VMEM),
        scratch_shapes=[
            pltpu.VMEM((n_col, long, width), f32),
            pltpu.SemaphoreType.DMA((n_col,)),
        ],
        compiler_params=pltpu.CompilerParams(vmem_limit_bytes=12 << 20),
        cost_estimate=estimate(8 * rows_here * blocks * width, 8 * rows_here * blocks * width),
        name="stage",
    )(flat)

    def collect(hop, pieces, *state):
        shapes = [len(p) for p in pieces]
        return pl.pallas_call(
            functools.partial(collect_kernel, hop, n_col, shapes),
            out_shape=cross_shape,
            in_specs=[SMEM] + [VMEM] * (sum(shapes) + 2 + len(state)),
            out_specs=VMEM,
            compiler_params=pltpu.CompilerParams(vmem_limit_bytes=8 << 20),
            cost_estimate=estimate(
                6 * len(pieces) * rows * size * blocks * width,
                4 * len(pieces) * long * width,
            ),
            name="collect",
        )(where, *sum(pieces, []), *staged, *state)

    def factor(begin, *given):
        start = begin == 0
        return pl.pallas_call(
            functools.partial(factor_kernel, begin, begin + SPAN),
            out_shape=shape((size, size), f32),
            in_specs=[SMEM] + [VMEM] * len(given),
            out_specs=VMEM,
            scratch_shapes=[pltpu.VMEM((3 * width, width), f32)] if start else [],
            compiler_params=pltpu.CompilerParams(vmem_limit_bytes=8 << 20),
            cost_estimate=estimate(256 * size**3, 8 * size * size),
            name="factor",
        )(where, *given)

    up = [(c, (c + 1) % n_col) for c in range(n_col)]
    down = [(c, (c - 1) % n_col) for c in range(n_col)]
    flips = [[(c, c ^ bit) for c in range(n_col)] for bit in (4, 2, 1)]
    swap, along_x, along_y, chips = perms
    piece = hand_out(matrix[:, 0, 0, :], spots, hits, n_col)
    piece, *staged = lax.optimization_barrier((piece, *staged))
    gram = pl.pallas_call(
        gram_kernel,
        out_shape=shape((3, width, width), f32),
        in_specs=[VMEM],
        out_specs=VMEM,
        compiler_params=pltpu.CompilerParams(vmem_limit_bytes=8 << 20),
        cost_estimate=estimate(8 * rows * size * width, 4 * rows * size),
        name="gram",
    )(piece)
    every = [[piece]]

    left, right = lax.ppermute(piece, "col", up), lax.ppermute(piece, "col", down)
    pair = gram.reshape(2, -1, width)
    mine = pick(pair, this) + lax.ppermute(pick(pair, that), "row", swap)
    mine = mine.reshape(nx, -1, width)
    got = [lax.ppermute(pick(mine, steps[s + 1]), "row", p) for s, p in enumerate(along_x)]
    cross = collect(0, [[piece]])
    left, right, cross = lax.optimization_barrier((left, right, cross))
    every += [[left], [right]]

    left, right = lax.ppermute(left, "col", up), lax.ppermute(right, "col", down)
    mine = total(pick(mine, steps[0]), got)
    got = send(mine, along_y)
    cross = collect(1, every[1:3], cross)
    left, right, cross, mine = lax.optimization_barrier((left, right, cross, mine))
    every += [[left], [right]]

    left, right = lax.ppermute(left, "col", up), lax.ppermute(right, "col", down)
    mine = total(mine, got)
    mine = mine + lax.ppermute(mine, "col", flips[0])
    got = lax.ppermute(mine, "col", flips[1])
    cross = collect(2, every[3:5], cross)
    left, right, cross, mine, got = lax.optimization_barrier((left, right, cross, mine, got))
    every += [[left], [right]]

    last = [
        lax.ppermute(left[:rows], "col", up),
        lax.ppermute(right[rows:], "col", down),
    ]
    mine = mine + got
    mine = mine + lax.ppermute(mine, "col", flips[2])
    got = send(mine, along_x)
    cross = collect(3, every[5:7], cross)
    *last, cross, mine = lax.optimization_barrier((*last, cross, mine))
    every += [last]

    cross = collect(4, [last], cross)
    whole = cross.reshape(2, len(chips[0]), -1, width)
    part = pick(whole, this) + lax.ppermute(pick(whole, that), "row", swap)
    took = exchange(part, chips)
    mine = after(jnp.stack([mine, *got]), part)
    other = lax.ppermute(mine, "row", swap)
    work = factor(SPAN, factor(0, mine, other))
    part = jnp.broadcast_to(jnp.sum(took, axis=0), took.shape)
    part, work = lax.optimization_barrier((part, work))
    took = exchange(part, chips)
    work = factor(3 * SPAN, factor(2 * SPAN, work))
    cross_mine = after(took.reshape(-1, width), work)
    cross_other = lax.ppermute(cross_mine, "row", swap)
    shapes = [len(p) for p in every]
    scaled, residual = pl.pallas_call(
        functools.partial(
            residual_kernel, n_col, blocks, 1.0 / math.sqrt(rows_here * n_row), shapes
        ),
        out_shape=(
            shape((size * blocks, width), f32),
            shape((rows_here * blocks, width), f32),
        ),
        in_specs=[SMEM] + [VMEM] * sum(shapes) + [HBM, VMEM, VMEM, VMEM],
        out_specs=(VMEM, HBM),
        scratch_shapes=[
            pltpu.VMEM((n_col, long, width), f32),
            pltpu.VMEM((n_col, long, width), f32),
            pltpu.VMEM((size * blocks, width), f32),
            pltpu.VMEM((n_col, rows, size), jnp.bfloat16),
            pltpu.VMEM((n_col, rows, size), jnp.bfloat16),
            pltpu.SemaphoreType.DMA((n_col,)),
            pltpu.SemaphoreType.DMA((n_col,)),
        ],
        compiler_params=pltpu.CompilerParams(vmem_limit_bytes=28 << 20),
        cost_estimate=estimate(
            6 * rows_here * size * blocks * width, 4 * rows_here * (size + 2 * blocks * width)
        ),
        name="residual",
    )(where, *sum(every, []), flat, cross_mine, cross_other, work)
    return (
        scaled.reshape(size, blocks, 1, width),
        residual.reshape(rows_here, blocks, 1, width),
    )


def solution(mesh):
    return jax.shard_map(
        functools.partial(per_device, mesh.shape["row"], mesh.shape["col"]),
        mesh=mesh,
        in_specs=(P("row", None, "col", None),),
        out_specs=(P(None, None, "col", None), P("row", None, "col", None)),
        check_vma=False,
    )
```

```python
import functools
import math

import jax
import jax.numpy as jnp
from jax import lax
from jax.experimental import pallas as pl
from jax.experimental.pallas import tpu as pltpu
from jax.sharding import PartitionSpec as P

LANES = 128
STEP = 64
GROUP = 8
SPAN = 64
HIGHEST = lax.Precision.HIGHEST


def split(value):
    high = value.astype(jnp.bfloat16)
    low = (value - high.astype(jnp.float32)).astype(jnp.bfloat16)
    return high, low


def contract(left, right, dims, precision=None):
    return lax.dot_general(
        left, right, (dims, ((), ())), precision=precision, preferred_element_type=jnp.float32
    )


def dot3(left, right, dims):
    (lh, ll), (rh, rl) = left, right
    return contract(lh, rh, dims) + (contract(lh, rl, dims) + contract(ll, rh, dims))


def dot4(left, right, dims):
    return dot3(left, right, dims) + contract(left[1], right[1], dims)


def sources(col, hop, n_col):
    if hop == 0 or 2 * hop == n_col:
        return [lax.rem(col + hop, n_col)]
    return [lax.rem(col + n_col - hop, n_col), lax.rem(col + hop, n_col)]


def load_piece(refs):
    if len(refs) == 1:
        half = refs[0].shape[0] // 2
        return jnp.concatenate([refs[0][:half], refs[0][half:]], axis=1)
    return jnp.concatenate([refs[0][...], refs[1][...]], axis=1)


def fetch(matrix_ref, window_ref, sem, chunk, long):
    start = pl.multiple_of(chunk * long, long)
    return pltpu.make_async_copy(matrix_ref.at[pl.ds(start, long)], window_ref, sem)


def load_blocks(window_ref, rows, blocks):
    return jnp.concatenate(
        [window_ref[pl.ds(block, rows, stride=blocks), :] for block in range(blocks)], axis=1
    )


FIRST = ((0,), (0,))


def gram_kernel(piece_ref, gram_ref):
    half = piece_ref.shape[0] // 2
    left, right = split(piece_ref[:half]), split(piece_ref[half:])
    gram_ref[0] = dot4(left, left, FIRST)
    gram_ref[1] = dot4(right, right, FIRST)
    gram_ref[2] = dot4(left, right, FIRST)


def stage_kernel(blocks, matrix_ref, high_ref, low_ref, window, sems):
    chunks, long = window.shape[0], window.shape[1]
    rows = long // blocks
    copies = [fetch(matrix_ref, window.at[i], sems.at[i], i, long) for i in range(chunks)]
    for copy in copies:
        copy.start()

    def step(i, carry):
        fetch(matrix_ref, window.at[i], sems.at[i], i, long).wait()
        for b in range(blocks):
            high, low = split(window[i, pl.ds(b, rows, stride=blocks), :])
            high_ref[i, :, LANES * b : LANES * (b + 1)] = high
            low_ref[i, :, LANES * b : LANES * (b + 1)] = low
        return carry

    lax.fori_loop(0, chunks, step, 0)


def collect_kernel(hop, n_col, shapes, where_ref, *refs):
    pieces = []
    for count in shapes:
        pieces.append(refs[:count])
        refs = refs[count:]
    high_ref, low_ref, cross_ref = refs[0], refs[1], refs[-1]
    total = None
    for i, chunk in enumerate(sources(where_ref[0], hop, n_col)):
        panel = split(load_piece(pieces[i]))
        term = dot3(panel, (high_ref[chunk], low_ref[chunk]), FIRST)
        total = term if total is None else total + term
    for b in range(cross_ref.shape[0]):
        term = total[:, LANES * b : LANES * (b + 1)]
        cross_ref[b] = refs[2][b] + term if hop else term


def factor_kernel(begin, end, where_ref, *refs):
    if begin == 0:
        mine_ref, other_ref, work, parts = refs
        core = where_ref[1]
        count = mine_ref.shape[0]
        parts[pl.ds(pl.multiple_of(core * count, count), count)] = mine_ref[...]
        parts[pl.ds(pl.multiple_of((1 - core) * count, count), count)] = other_ref[...]
        work[:LANES, :LANES] = parts[:LANES]
        work[:LANES, LANES:] = parts[2 * LANES :]
        work[LANES:, :LANES] = jnp.zeros((LANES, LANES), jnp.float32)
        work[LANES:, LANES:] = parts[LANES : 2 * LANES]
    else:
        work_in, work = refs
        work[...] = work_in[...]
    size = work.shape[0]
    halves = size // LANES
    lane = lax.broadcasted_iota(jnp.int32, (8, LANES), 1)
    sub = lax.broadcasted_iota(jnp.int32, (8, LANES), 0)
    wide = (8, LANES)
    for begin in range(begin, end, STEP):
        tiles = [
            [work[begin + 8 * t : begin + 8 * t + 8, LANES * h : LANES * (h + 1)] for h in range(halves)]
            for t in range(STEP // 8)
        ]
        hot = begin // LANES
        for j in range(0, STEP, GROUP):
            t0, r0 = j // 8, j % 8
            l0 = (begin + j) % LANES
            below = range(t0, STEP // 8)
            cols = [
                {t: jnp.broadcast_to(tiles[t][hot][:, l0 + q : l0 + q + 1], wide) for t in below}
                for q in range(GROUP)
            ]
            rows = [
                [jnp.broadcast_to(tiles[t0][h][r0 + q : r0 + q + 1], wide) for h in range(halves)]
                for q in range(GROUP)
            ]
            small = {
                (i, q): jnp.broadcast_to(cols[q][t0][r0 + i : r0 + i + 1], wide)
                for q in range(GROUP)
                for i in range(q, GROUP)
            }
            for q in range(GROUP):
                inv = lax.rsqrt(small[q, q])
                at = lane == l0 + q
                rows[q] = [v * inv for v in rows[q]]
                rows[q][hot] = jnp.where(at, inv, rows[q][hot])
                cols[q] = {t: v * inv for t, v in cols[q].items()}
                ell = {i: small[i, q] * inv for i in range(q + 1, GROUP)}
                for i in range(q + 1, GROUP):
                    for p in range(q + 1, i + 1):
                        small[i, p] = small[i, p] - ell[i] * ell[p]
                    rows[i][hot] = jnp.where(at, 0.0, rows[i][hot])
                    rows[i] = [v - ell[i] * u for v, u in zip(rows[i], rows[q])]
                    cols[i] = {t: v - cols[q][t] * ell[i] for t, v in cols[i].items()}
            cleared = jnp.logical_and(lane >= l0, lane < l0 + GROUP)
            for q in range(GROUP - 1):
                stale = jnp.logical_and(lane > l0 + q, lane < l0 + GROUP)
                rows[q][hot] = jnp.where(stale, 0.0, rows[q][hot])
            for t in below:
                fresh = []
                for h in range(halves):
                    value = tiles[t][h]
                    if h == hot:
                        value = jnp.where(cleared, 0.0, value)
                    for q in range(GROUP):
                        value = value - cols[q][t] * rows[q][h]
                    if t == t0:
                        value = jnp.where(sub < r0, tiles[t][h], value)
                        for q in range(GROUP):
                            value = jnp.where(sub == r0 + q, rows[q][h], value)
                    fresh.append(value)
                tiles[t] = fresh
        panel = jnp.concatenate([jnp.concatenate(t, axis=1) for t in tiles], axis=0)
        column = lax.broadcasted_iota(jnp.int32, (STEP, size), 1)
        line = lax.broadcasted_iota(jnp.int32, (STEP, size), 0) + begin
        upper = jnp.logical_and(column > line, column < begin + STEP)
        panel = jnp.where(upper, 0.0, panel)
        if begin + STEP < size:
            base = (begin + STEP) // LANES * LANES
            ahead = jnp.where(column >= begin + STEP, panel, 0.0)[:, base:]
            update = contract(ahead, panel, ((0,), (0,)), HIGHEST)
            here = lax.broadcasted_iota(jnp.int32, (size - base, size), 1)
            old = jnp.where(jnp.logical_and(here >= begin, here < begin + STEP), 0.0, work[base:, :])
            work[base:, :] = old - update
        work[begin : begin + STEP, :] = jnp.where(column < begin + STEP, panel, 0.0)


def residual_kernel(n_col, blocks, scale, shapes, where_ref, *refs):
    pieces = []
    for count in shapes:
        pieces.append(refs[:count])
        refs = refs[count:]
    matrix_ref, mine_ref, other_ref, inverse_ref = refs[:4]
    rows_ref, out_ref, window, result, cross, high, low, sems, out_sems = refs[4:]
    col, core, x = where_ref[0], where_ref[1], where_ref[2]
    chunks, long = window.shape[0], window.shape[1]
    rows = long // blocks
    for i in range(chunks):
        fetch(matrix_ref, window.at[i], sems.at[i], i, long).start()
    order = sum([sources(col, hop, n_col) for hop in range(n_col // 2 + 1)], [])
    for piece, chunk in zip(pieces, order):
        high[chunk], low[chunk] = split(load_piece(piece))
    quarters, quarter = mine_ref.shape[0], mine_ref.shape[1]
    for hop in range(quarters):
        spot = lax.rem(x + quarters - hop, quarters)
        base = pl.multiple_of((core * quarters + spot) * quarter, quarter)
        cross[pl.ds(base, quarter)] = mine_ref[hop]
        base = pl.multiple_of(((1 - core) * quarters + spot) * quarter, quarter)
        cross[pl.ds(base, quarter)] = other_ref[hop]
    inverse = inverse_ref[...]
    size = inverse.shape[0]
    every = jnp.concatenate([cross[size * b : size * (b + 1)] for b in range(blocks)], axis=1)
    top = contract(inverse, every, ((1,), (0,)), HIGHEST)
    weights = split(contract(inverse, top, FIRST, HIGHEST))
    for block in range(blocks):
        rows_ref[pl.ds(block, size, stride=blocks), :] = (
            top[:, LANES * block : LANES * (block + 1)] * scale
        )
    high_weights, low_weights = weights

    def write(i):
        start = pl.multiple_of(i * long, long)
        return pltpu.make_async_copy(
            result.at[i], out_ref.at[pl.ds(start, long)], out_sems.at[i]
        )

    def step(i, carry):
        fit = dot3((high[i], low[i]), (high_weights, low_weights), ((1,), (0,)))
        fetch(matrix_ref, window.at[i], sems.at[i], i, long).wait()
        for block in range(blocks):
            result[i, pl.ds(block, rows, stride=blocks), :] = (
                window[i, pl.ds(block, rows, stride=blocks), :]
                - fit[:, LANES * block : LANES * (block + 1)]
            )
        write(i).start()
        return carry

    lax.fori_loop(0, chunks, step, 0)
    for i in range(chunks):
        write(i).wait()


VMEM = pl.BlockSpec(memory_space=pltpu.VMEM)
ANY = pl.BlockSpec(memory_space=pl.ANY)
HBM = pl.BlockSpec(memory_space=pltpu.HBM)
SMEM = pl.BlockSpec(memory_space=pltpu.SMEM)


def pick(value, index):
    return lax.dynamic_index_in_dim(value, index, 0, keepdims=False)


def row_perms(n_row):
    nx = ny = math.isqrt(n_row // 2)

    def rank(x, y, core):
        return (x % nx * ny + y % ny) * 2 + core

    def table(dx, dy, flip):
        return [
            (rank(x, y, core), rank(x + dx, y + dy, core ^ flip))
            for x in range(nx)
            for y in range(ny)
            for core in range(2)
        ]

    return (
        table(0, 0, 1),
        [table(s, 0, 0) for s in range(1, nx)],
        [table(0, s, 0) for s in range(1, ny)],
    )


def send(value, perms):
    return [lax.ppermute(value, "row", perm) for perm in perms]


def total(value, got):
    return (value + got[1]) + (got[0] + got[2])


def hand_out(own, spots, hits, n_col):
    pieces = own.reshape(n_col, -1, LANES)
    first, second = pieces[0], pieces[1]
    for s in range(1, n_col):
        pairs = [(0, s), (1, (1 + s) % n_col)]
        got = lax.ppermute(pick(pieces, spots[s]), "col", pairs)
        first = jnp.where(hits[s], got, first)
        second = jnp.where(hits[(1 + s) % n_col], got, second)
    return jnp.concatenate([first, second])


def after(value, *done):
    return lax.optimization_barrier((value, *done))[0]


def estimate(flops, moved):
    return pl.CostEstimate(flops=flops, bytes_accessed=moved, transcendentals=0)


def per_device(n_row, n_col, matrix):
    rows_here, blocks, _, width = matrix.shape
    col = lax.axis_index("col")
    row = lax.axis_index("row")
    perms = row_perms(n_row)
    nx = len(perms[1]) + 1
    core = lax.rem(row, 2)
    x = row // (n_row // nx)
    where = jnp.stack([col, core, x]).astype(jnp.int32)
    unsigned = jnp.uint32
    spots = [lax.rem(col + s, n_col).astype(unsigned) for s in range(n_col)]
    hits = [col == s for s in range(n_col)]
    steps = [lax.rem(x + s, nx).astype(unsigned) for s in range(nx)]
    this, that = core.astype(unsigned), (1 - core).astype(unsigned)
    matrix, where, spots, hits, steps, this, that = lax.optimization_barrier(
        (matrix, where, spots, hits, steps, this, that)
    )
    flat = matrix.reshape(rows_here * blocks, width)
    size = 2 * width
    rows = rows_here // n_col
    long = rows * blocks
    f32 = jnp.float32
    shape = jax.ShapeDtypeStruct
    flat = pltpu.with_memory_space_constraint(flat, pltpu.HBM)
    cross_shape = shape((blocks, size, width), f32)

    parts = (shape((n_col, rows, blocks * width), jnp.bfloat16),) * 2
    staged = pl.pallas_call(
        functools.partial(stage_kernel, blocks),
        out_shape=parts,
        in_specs=[HBM],
        out_specs=(VMEM, VMEM),
        scratch_shapes=[
            pltpu.VMEM((n_col, long, width), f32),
            pltpu.SemaphoreType.DMA((n_col,)),
        ],
        compiler_params=pltpu.CompilerParams(vmem_limit_bytes=12 << 20),
        cost_estimate=estimate(8 * rows_here * blocks * width, 8 * rows_here * blocks * width),
        name="stage",
    )(flat)

    def collect(hop, pieces, *state):
        shapes = [len(p) for p in pieces]
        return pl.pallas_call(
            functools.partial(collect_kernel, hop, n_col, shapes),
            out_shape=cross_shape,
            in_specs=[SMEM] + [VMEM] * (sum(shapes) + 2 + len(state)),
            out_specs=VMEM,
            compiler_params=pltpu.CompilerParams(vmem_limit_bytes=8 << 20),
            cost_estimate=estimate(
                6 * len(pieces) * rows * size * blocks * width,
                4 * len(pieces) * long * width,
            ),
            name="collect",
        )(where, *sum(pieces, []), *staged, *state)

    def factor(begin, *given):
        start = begin == 0
        return pl.pallas_call(
            functools.partial(factor_kernel, begin, begin + SPAN),
            out_shape=shape((size, size), f32),
            in_specs=[SMEM] + [VMEM] * len(given),
            out_specs=VMEM,
            scratch_shapes=[pltpu.VMEM((3 * width, width), f32)] if start else [],
            compiler_params=pltpu.CompilerParams(vmem_limit_bytes=8 << 20),
            cost_estimate=estimate(256 * size**3, 8 * size * size),
            name="factor",
        )(where, *given)

    up = [(c, (c + 1) % n_col) for c in range(n_col)]
    down = [(c, (c - 1) % n_col) for c in range(n_col)]
    flips = [[(c, c ^ bit) for c in range(n_col)] for bit in (4, 2, 1)]
    swap, along_x, along_y = perms
    piece = hand_out(matrix[:, 0, 0, :], spots, hits, n_col)
    piece, *staged = lax.optimization_barrier((piece, *staged))
    gram = pl.pallas_call(
        gram_kernel,
        out_shape=shape((3, width, width), f32),
        in_specs=[VMEM],
        out_specs=VMEM,
        compiler_params=pltpu.CompilerParams(vmem_limit_bytes=8 << 20),
        cost_estimate=estimate(8 * rows * size * width, 4 * rows * size),
        name="gram",
    )(piece)
    every = [[piece]]

    left, right = lax.ppermute(piece, "col", up), lax.ppermute(piece, "col", down)
    pair = gram.reshape(2, -1, width)
    mine = pick(pair, this) + lax.ppermute(pick(pair, that), "row", swap)
    got = send(mine, along_x)
    cross = collect(0, [[piece]])
    left, right, cross = lax.optimization_barrier((left, right, cross))
    every += [[left], [right]]

    left, right = lax.ppermute(left, "col", up), lax.ppermute(right, "col", down)
    mine = total(mine, got)
    got = send(mine, along_y)
    cross = collect(1, every[1:3], cross)
    left, right, cross, mine = lax.optimization_barrier((left, right, cross, mine))
    every += [[left], [right]]

    left, right = lax.ppermute(left, "col", up), lax.ppermute(right, "col", down)
    mine = total(mine, got)
    got = lax.ppermute(mine, "col", flips[0])
    cross = collect(2, every[3:5], cross)
    left, right, cross, mine = lax.optimization_barrier((left, right, cross, mine))
    every += [[left], [right]]

    last = [
        lax.ppermute(left[:rows], "col", up),
        lax.ppermute(right[rows:], "col", down),
    ]
    mine = mine + got
    got = lax.ppermute(mine, "col", flips[1])
    cross = collect(3, every[5:7], cross)
    *last, cross, mine, got = lax.optimization_barrier((*last, cross, mine, got))
    every += [last]

    mine = mine + got
    got = lax.ppermute(mine, "col", flips[2])
    cross = collect(4, [last], cross)
    whole = cross.reshape(2, nx, -1, width)
    part = pick(whole, this) + lax.ppermute(pick(whole, that), "row", swap)
    took = [
        lax.ppermute(pick(part, steps[s + 1]), "row", p) for s, p in enumerate(along_x)
    ]
    mine = mine + after(got, part)
    other = lax.ppermute(mine, "row", swap)
    part = total(pick(part, steps[0]), took)
    took = send(part, along_y)
    work = factor(SPAN, factor(0, mine, after(other, part)))
    part = after(total(part, took), work)
    took = send(part, along_x)
    work = factor(3 * SPAN, factor(2 * SPAN, after(work, part)))
    cross_mine = after(jnp.stack([part, *took]), work)
    cross_other = lax.ppermute(cross_mine, "row", swap)
    shapes = [len(p) for p in every]
    scaled, residual = pl.pallas_call(
        functools.partial(
            residual_kernel, n_col, blocks, 1.0 / math.sqrt(rows_here * n_row), shapes
        ),
        out_shape=(
            shape((size * blocks, width), f32),
            shape((rows_here * blocks, width), f32),
        ),
        in_specs=[SMEM] + [VMEM] * sum(shapes) + [HBM, VMEM, VMEM, VMEM],
        out_specs=(VMEM, HBM),
        scratch_shapes=[
            pltpu.VMEM((n_col, long, width), f32),
            pltpu.VMEM((n_col, long, width), f32),
            pltpu.VMEM((size * blocks, width), f32),
            pltpu.VMEM((n_col, rows, size), jnp.bfloat16),
            pltpu.VMEM((n_col, rows, size), jnp.bfloat16),
            pltpu.SemaphoreType.DMA((n_col,)),
            pltpu.SemaphoreType.DMA((n_col,)),
        ],
        compiler_params=pltpu.CompilerParams(vmem_limit_bytes=28 << 20),
        cost_estimate=estimate(
            6 * rows_here * size * blocks * width, 4 * rows_here * (size + 2 * blocks * width)
        ),
        name="residual",
    )(where, *sum(every, []), flat, cross_mine, cross_other, work)
    return (
        scaled.reshape(size, blocks, 1, width),
        residual.reshape(rows_here, blocks, 1, width),
    )


def solution(mesh):
    return jax.shard_map(
        functools.partial(per_device, mesh.shape["row"], mesh.shape["col"]),
        mesh=mesh,
        in_specs=(P("row", None, "col", None),),
        out_specs=(P(None, None, "col", None), P("row", None, "col", None)),
        check_vma=False,
    )
```

```python
import functools
import math

import jax
import jax.numpy as jnp
from jax import lax
from jax.experimental import pallas as pl
from jax.experimental.pallas import tpu as pltpu
from jax.sharding import PartitionSpec as P

LANES = 128
STEP = 64
GROUP = 8
SPAN = 64
HIGHEST = lax.Precision.HIGHEST


def split(value):
    high = value.astype(jnp.bfloat16)
    low = (value - high.astype(jnp.float32)).astype(jnp.bfloat16)
    return high, low


def contract(left, right, dims, precision=None):
    return lax.dot_general(
        left, right, (dims, ((), ())), precision=precision, preferred_element_type=jnp.float32
    )


def dot3(left, right, dims):
    (lh, ll), (rh, rl) = left, right
    return contract(lh, rh, dims) + (contract(lh, rl, dims) + contract(ll, rh, dims))


def dot4(left, right, dims):
    return dot3(left, right, dims) + contract(left[1], right[1], dims)


def load_piece(ref, chunk):
    half = ref.shape[1] // 2
    return jnp.concatenate([ref[chunk, :half], ref[chunk, half:]], axis=1)


def fetch(matrix_ref, window_ref, sem, chunk, long):
    start = pl.multiple_of(chunk * long, long)
    return pltpu.make_async_copy(matrix_ref.at[pl.ds(start, long)], window_ref, sem)


FIRST = ((0,), (0,))


def gram_kernel(piece_ref, gram_ref):
    half = piece_ref.shape[0] // 2
    left, right = split(piece_ref[:half]), split(piece_ref[half:])
    gram_ref[0] = dot4(left, left, FIRST)
    gram_ref[1] = dot4(right, right, FIRST)
    gram_ref[2] = dot4(left, right, FIRST)


def stage_kernel(blocks, matrix_ref, high_ref, low_ref, window, sems):
    chunks, long = window.shape[0], window.shape[1]
    rows = long // blocks
    copies = [fetch(matrix_ref, window.at[i], sems.at[i], i, long) for i in range(chunks)]
    for copy in copies:
        copy.start()

    def step(i, carry):
        fetch(matrix_ref, window.at[i], sems.at[i], i, long).wait()
        for b in range(blocks):
            high, low = split(window[i, pl.ds(b, rows, stride=blocks), :])
            high_ref[i, :, LANES * b : LANES * (b + 1)] = high
            low_ref[i, :, LANES * b : LANES * (b + 1)] = low
        return carry

    lax.fori_loop(0, chunks, step, 0)


def collect_kernel(panel_ref, high_ref, low_ref, cross_ref):
    cross_ref[...] = jnp.zeros_like(cross_ref)

    def step(i, carry):
        term = dot3(split(load_piece(panel_ref, i)), (high_ref[i], low_ref[i]), FIRST)
        for b in range(cross_ref.shape[0]):
            cross_ref[b] += term[:, LANES * b : LANES * (b + 1)]
        return carry

    lax.fori_loop(0, panel_ref.shape[0], step, 0)


def factor_kernel(begin, end, where_ref, *refs):
    if begin == 0:
        mine_ref, other_ref, work, parts = refs
        core = where_ref[1]
        count = mine_ref.shape[0]
        parts[pl.ds(pl.multiple_of(core * count, count), count)] = mine_ref[...]
        parts[pl.ds(pl.multiple_of((1 - core) * count, count), count)] = other_ref[...]
        work[:LANES, :LANES] = parts[:LANES]
        work[:LANES, LANES:] = parts[2 * LANES :]
        work[LANES:, :LANES] = jnp.zeros((LANES, LANES), jnp.float32)
        work[LANES:, LANES:] = parts[LANES : 2 * LANES]
    else:
        work_in, work = refs
        work[...] = work_in[...]
    size = work.shape[0]
    halves = size // LANES
    lane = lax.broadcasted_iota(jnp.int32, (8, LANES), 1)
    sub = lax.broadcasted_iota(jnp.int32, (8, LANES), 0)
    wide = (8, LANES)
    for begin in range(begin, end, STEP):
        tiles = [
            [work[begin + 8 * t : begin + 8 * t + 8, LANES * h : LANES * (h + 1)] for h in range(halves)]
            for t in range(STEP // 8)
        ]
        hot = begin // LANES
        for j in range(0, STEP, GROUP):
            t0, r0 = j // 8, j % 8
            l0 = (begin + j) % LANES
            below = range(t0, STEP // 8)
            cols = [
                {t: jnp.broadcast_to(tiles[t][hot][:, l0 + q : l0 + q + 1], wide) for t in below}
                for q in range(GROUP)
            ]
            rows = [
                [jnp.broadcast_to(tiles[t0][h][r0 + q : r0 + q + 1], wide) for h in range(halves)]
                for q in range(GROUP)
            ]
            small = {
                (i, q): jnp.broadcast_to(cols[q][t0][r0 + i : r0 + i + 1], wide)
                for q in range(GROUP)
                for i in range(q, GROUP)
            }
            for q in range(GROUP):
                inv = lax.rsqrt(small[q, q])
                at = lane == l0 + q
                rows[q] = [v * inv for v in rows[q]]
                rows[q][hot] = jnp.where(at, inv, rows[q][hot])
                cols[q] = {t: v * inv for t, v in cols[q].items()}
                ell = {i: small[i, q] * inv for i in range(q + 1, GROUP)}
                for i in range(q + 1, GROUP):
                    for p in range(q + 1, i + 1):
                        small[i, p] = small[i, p] - ell[i] * ell[p]
                    rows[i][hot] = jnp.where(at, 0.0, rows[i][hot])
                    rows[i] = [v - ell[i] * u for v, u in zip(rows[i], rows[q])]
                    cols[i] = {t: v - cols[q][t] * ell[i] for t, v in cols[i].items()}
            cleared = jnp.logical_and(lane >= l0, lane < l0 + GROUP)
            for q in range(GROUP - 1):
                stale = jnp.logical_and(lane > l0 + q, lane < l0 + GROUP)
                rows[q][hot] = jnp.where(stale, 0.0, rows[q][hot])
            for t in below:
                fresh = []
                for h in range(halves):
                    value = tiles[t][h]
                    if h == hot:
                        value = jnp.where(cleared, 0.0, value)
                    for q in range(GROUP):
                        value = value - cols[q][t] * rows[q][h]
                    if t == t0:
                        value = jnp.where(sub < r0, tiles[t][h], value)
                        for q in range(GROUP):
                            value = jnp.where(sub == r0 + q, rows[q][h], value)
                    fresh.append(value)
                tiles[t] = fresh
        panel = jnp.concatenate([jnp.concatenate(t, axis=1) for t in tiles], axis=0)
        column = lax.broadcasted_iota(jnp.int32, (STEP, size), 1)
        line = lax.broadcasted_iota(jnp.int32, (STEP, size), 0) + begin
        upper = jnp.logical_and(column > line, column < begin + STEP)
        panel = jnp.where(upper, 0.0, panel)
        if begin + STEP < size:
            base = (begin + STEP) // LANES * LANES
            ahead = jnp.where(column >= begin + STEP, panel, 0.0)[:, base:]
            update = contract(ahead, panel, ((0,), (0,)), HIGHEST)
            here = lax.broadcasted_iota(jnp.int32, (size - base, size), 1)
            old = jnp.where(jnp.logical_and(here >= begin, here < begin + STEP), 0.0, work[base:, :])
            work[base:, :] = old - update
        work[begin : begin + STEP, :] = jnp.where(column < begin + STEP, panel, 0.0)


def residual_kernel(blocks, scale, where_ref, *refs):
    panel_ref, matrix_ref, mine_ref, other_ref, inverse_ref = refs[:5]
    rows_ref, out_ref, window, result, cross, sems, out_sems = refs[5:]
    core, x = where_ref[1], where_ref[2]
    chunks, long = window.shape[0], window.shape[1]
    rows = long // blocks
    for i in range(chunks):
        fetch(matrix_ref, window.at[i], sems.at[i], i, long).start()
    quarters, quarter = mine_ref.shape[0], mine_ref.shape[1]
    for hop in range(quarters):
        spot = lax.rem(x + quarters - hop, quarters)
        base = pl.multiple_of((core * quarters + spot) * quarter, quarter)
        cross[pl.ds(base, quarter)] = mine_ref[hop]
        base = pl.multiple_of(((1 - core) * quarters + spot) * quarter, quarter)
        cross[pl.ds(base, quarter)] = other_ref[hop]
    inverse = inverse_ref[...]
    size = inverse.shape[0]
    every = jnp.concatenate([cross[size * b : size * (b + 1)] for b in range(blocks)], axis=1)
    top = contract(inverse, every, ((1,), (0,)), HIGHEST)
    weights = split(contract(inverse, top, FIRST, HIGHEST))
    for block in range(blocks):
        rows_ref[pl.ds(block, size, stride=blocks), :] = (
            top[:, LANES * block : LANES * (block + 1)] * scale
        )
    high_weights, low_weights = weights

    def write(i):
        start = pl.multiple_of(i * long, long)
        return pltpu.make_async_copy(
            result.at[i], out_ref.at[pl.ds(start, long)], out_sems.at[i]
        )

    def step(i, carry):
        panel = split(load_piece(panel_ref, i))
        fit = dot3(panel, (high_weights, low_weights), ((1,), (0,)))
        fetch(matrix_ref, window.at[i], sems.at[i], i, long).wait()
        for block in range(blocks):
            result[i, pl.ds(block, rows, stride=blocks), :] = (
                window[i, pl.ds(block, rows, stride=blocks), :]
                - fit[:, LANES * block : LANES * (block + 1)]
            )
        write(i).start()
        return carry

    lax.fori_loop(0, chunks, step, 0)
    for i in range(chunks):
        write(i).wait()


VMEM = pl.BlockSpec(memory_space=pltpu.VMEM)
ANY = pl.BlockSpec(memory_space=pl.ANY)
HBM = pl.BlockSpec(memory_space=pltpu.HBM)
SMEM = pl.BlockSpec(memory_space=pltpu.SMEM)


def pick(value, index):
    return lax.dynamic_index_in_dim(value, index, 0, keepdims=False)


def row_perms(n_row):
    nx = ny = math.isqrt(n_row // 2)

    def rank(x, y, core):
        return (x % nx * ny + y % ny) * 2 + core

    def table(dx, dy, flip):
        return [
            (rank(x, y, core), rank(x + dx, y + dy, core ^ flip))
            for x in range(nx)
            for y in range(ny)
            for core in range(2)
        ]

    return (
        table(0, 0, 1),
        [table(s, 0, 0) for s in range(1, nx)],
        [table(0, s, 0) for s in range(1, ny)],
    )


def send(value, perms):
    return [lax.ppermute(value, "row", perm) for perm in perms]


def total(value, got):
    return (value + got[1]) + (got[0] + got[2])


def hand_out(own, spots, hits, n_col):
    pieces = own.reshape(n_col, -1, LANES)
    first, second = pieces[0], pieces[1]
    for s in range(1, n_col):
        pairs = [(0, s), (1, (1 + s) % n_col)]
        got = lax.ppermute(pick(pieces, spots[s]), "col", pairs)
        first = jnp.where(hits[s], got, first)
        second = jnp.where(hits[(1 + s) % n_col], got, second)
    return jnp.concatenate([first, second])


def after(value, *done):
    return lax.optimization_barrier((value, *done))[0]


def estimate(flops, moved):
    return pl.CostEstimate(flops=flops, bytes_accessed=moved, transcendentals=0)


def per_device(n_row, n_col, matrix):
    rows_here, blocks, _, width = matrix.shape
    col = lax.axis_index("col")
    row = lax.axis_index("row")
    perms = row_perms(n_row)
    nx = len(perms[1]) + 1
    core = lax.rem(row, 2)
    x = row // (n_row // nx)
    where = jnp.stack([col, core, x]).astype(jnp.int32)
    unsigned = jnp.uint32
    spots = [lax.rem(col + s, n_col).astype(unsigned) for s in range(n_col)]
    hits = [col == s for s in range(n_col)]
    steps = [lax.rem(x + s, nx).astype(unsigned) for s in range(nx)]
    this, that = core.astype(unsigned), (1 - core).astype(unsigned)
    matrix, where, spots, hits, steps, this, that = lax.optimization_barrier(
        (matrix, where, spots, hits, steps, this, that)
    )
    flat = matrix.reshape(rows_here * blocks, width)
    size = 2 * width
    rows = rows_here // n_col
    long = rows * blocks
    f32 = jnp.float32
    shape = jax.ShapeDtypeStruct
    flat = pltpu.with_memory_space_constraint(flat, pltpu.HBM)
    cross_shape = shape((blocks, size, width), f32)

    parts = (shape((n_col, rows, blocks * width), jnp.bfloat16),) * 2
    staged = pl.pallas_call(
        functools.partial(stage_kernel, blocks),
        out_shape=parts,
        in_specs=[HBM],
        out_specs=(VMEM, VMEM),
        scratch_shapes=[
            pltpu.VMEM((n_col, long, width), f32),
            pltpu.SemaphoreType.DMA((n_col,)),
        ],
        compiler_params=pltpu.CompilerParams(vmem_limit_bytes=12 << 20),
        cost_estimate=estimate(8 * rows_here * blocks * width, 8 * rows_here * blocks * width),
        name="stage",
    )(flat)

    def factor(begin, *given):
        start = begin == 0
        return pl.pallas_call(
            functools.partial(factor_kernel, begin, begin + SPAN),
            out_shape=shape((size, size), f32),
            in_specs=[SMEM] + [VMEM] * len(given),
            out_specs=VMEM,
            scratch_shapes=[pltpu.VMEM((3 * width, width), f32)] if start else [],
            compiler_params=pltpu.CompilerParams(vmem_limit_bytes=8 << 20),
            cost_estimate=estimate(256 * size**3, 8 * size * size),
            name="factor",
        )(where, *given)

    flips = [[(c, c ^ bit) for c in range(n_col)] for bit in (4, 2, 1)]
    swap, along_x, along_y = perms
    piece = hand_out(matrix[:, 0, 0, :], spots, hits, n_col)
    piece, *staged = lax.optimization_barrier((piece, *staged))
    gram = pl.pallas_call(
        gram_kernel,
        out_shape=shape((3, width, width), f32),
        in_specs=[VMEM],
        out_specs=VMEM,
        compiler_params=pltpu.CompilerParams(vmem_limit_bytes=8 << 20),
        cost_estimate=estimate(8 * rows * size * width, 4 * rows * size),
        name="gram",
    )(piece)
    panel = lax.all_gather(piece, "col")
    pair = gram.reshape(2, -1, width)
    mine = pick(pair, this) + lax.ppermute(pick(pair, that), "row", swap)
    mine = total(mine, send(mine, along_x))
    mine = total(mine, send(mine, along_y))
    for flip in flips:
        mine = mine + lax.ppermute(mine, "col", flip)
    other = lax.ppermute(mine, "row", swap)
    work = factor(0, mine, other)
    work = factor(SPAN, work)
    panel, work = lax.optimization_barrier((panel, work))
    cross = pl.pallas_call(
        collect_kernel,
        out_shape=cross_shape,
        in_specs=[VMEM] * 3,
        out_specs=VMEM,
        compiler_params=pltpu.CompilerParams(vmem_limit_bytes=12 << 20),
        cost_estimate=estimate(
            6 * rows_here * size * blocks * width, 4 * rows_here * (size + blocks * width)
        ),
        name="collect",
    )(panel, *staged)
    whole = cross.reshape(2, nx, -1, width)
    part = pick(whole, this) + lax.ppermute(pick(whole, that), "row", swap)
    took = [
        lax.ppermute(pick(part, steps[s + 1]), "row", p) for s, p in enumerate(along_x)
    ]
    part = total(pick(part, steps[0]), took)
    took = send(part, along_y)
    work = factor(2 * SPAN, after(work, part))
    part = after(total(part, took), work)
    took = send(part, along_x)
    work = factor(3 * SPAN, after(work, part))
    cross_mine = after(jnp.stack([part, *took]), work)
    cross_other = lax.ppermute(cross_mine, "row", swap)
    scaled, residual = pl.pallas_call(
        functools.partial(residual_kernel, blocks, 1.0 / math.sqrt(rows_here * n_row)),
        out_shape=(
            shape((size * blocks, width), f32),
            shape((rows_here * blocks, width), f32),
        ),
        in_specs=[SMEM, VMEM, HBM, VMEM, VMEM, VMEM],
        out_specs=(VMEM, HBM),
        scratch_shapes=[
            pltpu.VMEM((n_col, long, width), f32),
            pltpu.VMEM((n_col, long, width), f32),
            pltpu.VMEM((size * blocks, width), f32),
            pltpu.SemaphoreType.DMA((n_col,)),
            pltpu.SemaphoreType.DMA((n_col,)),
        ],
        compiler_params=pltpu.CompilerParams(vmem_limit_bytes=28 << 20),
        cost_estimate=estimate(
            6 * rows_here * size * blocks * width, 4 * rows_here * (size + 2 * blocks * width)
        ),
        name="residual",
    )(where, panel, flat, cross_mine, cross_other, work)
    return (
        scaled.reshape(size, blocks, 1, width),
        residual.reshape(rows_here, blocks, 1, width),
    )


def solution(mesh):
    return jax.shard_map(
        functools.partial(per_device, mesh.shape["row"], mesh.shape["col"]),
        mesh=mesh,
        in_specs=(P("row", None, "col", None),),
        out_specs=(P(None, None, "col", None), P("row", None, "col", None)),
        check_vma=False,
    )
```
